256 devices in a mesh: vol: 16 (over z_hi, y, core), sec: 16 (over z_lo, x).
Axes of the slice: x: 4, y: 4, z: 8 (z_hi: 2, z_lo: 4; z = z_hi * 4 + z_lo), core: 2. Of those that a mesh axis runs over, the one named last changes fastest.
Arguments:
- rhs: float32 [64, 8, 64, 2048], P(None, None, 'vol', 'sec'), may hold values from -6 to 6
- flux_in: float32 [64, 64, 2048], P(None, 'vol', 'sec'), may hold values from -12 to 12
- materials: int32 [8, 64, 2048], P(None, 'vol', 'sec'), may hold values from 0 to 7
- mat_coef: float32 [8], replicated, may hold values from 0.5 to 4
- owner_perm: int32 [16], replicated, may hold values from 0 to 15, each once
- blocks: bfloat16 [16, 8192, 8192], P('sec', None, 'vol'), may hold values from -0.0625 to 0.0625
Outputs:
- solution: float32 [64, 8, 64, 2048], P(None, None, 'vol', 'sec')
- flux_out: float32 [64, 64, 2048], P(None, 'vol', 'sec')
The draws below stay inside these ranges and needn't reach their ends.
Inputs may be any that keep to these rules, and one draw needn't show every extreme that they name: `owner_perm`: every harmonic index appears once.
All inputs are finite; a program needn't handle non-finite values.
Results may differ from the reference program's by a relative error of at most 0.008.
Values may be sent and summed in bfloat16 or wider, within the bound.
No kernel may reach another device: no remote copies, remote signals or barrier semaphores. Data moves between devices by JAX's collectives and lax.ppermute only.
A program may use at most 64 MiB of HBM per device.

```python
import math
import jax
import jax.numpy as jnp
from jax import lax

ORDER = 8192
PTS = 128
EXC = 64
DEPTH = 8
SWEEPS = 4
NMAT = 8
SECTORS = 16
NZ = 64
NA = 2048


def place_ends(values, rng, smallest, top_value):
    longest = values.shape.index(max(values.shape))
    spots = []
    for shift in (0, 1):
        where = [jax.random.randint(jax.random.fold_in(rng, axis), (), 0, length) for axis, length in enumerate(values.shape)]
        where[longest] = (where[longest] + shift) % values.shape[longest]
        spots.append(tuple(where))
    return values.at[spots[0]].set(smallest).at[spots[1]].set(top_value)


def shard_levels(own_key, shape, cuts, smallest, largest):
    def one(dim, parts):
        heights = jax.random.uniform(jax.random.fold_in(jax.random.fold_in(own_key, 6), dim), (parts,), jnp.float32, smallest / len(cuts), largest / len(cuts))
        return jnp.repeat(jnp.exp(heights), shape[dim] // parts).reshape((-1,) + (1,) * (len(shape) - dim - 1))

    factor_of = one(*cuts[0])
    for cut in cuts[1:]:
        factor_of = factor_of * one(*cut)
    return factor_of


def gaussian(own_key, extent, width, reach, split=(), held_as=jnp.bfloat16):
    values = jax.random.normal(own_key, extent, jnp.float32) * width
    if len(split) > 0:
        values = shard_levels(own_key, extent, split, -0.22, 0.18) * values
    return jnp.clip(values, min=-reach, max=reach).astype(held_as)


def setup_inputs(seed: int = 0) -> dict:
    key_of = jax.random.split(jax.random.key(seed), 7)
    rhs = gaussian(key_of[0], (EXC, DEPTH, NZ, NA), 1.0, 6.0, ((2, 16), (3, 16)), jnp.float32)
    flux_in = gaussian(key_of[1], (EXC, NZ, NA), 2.0, 12.0, ((1, 16), (2, 16)), jnp.float32)
    materials = place_ends(jax.random.randint(key_of[2], (DEPTH, NZ, NA), 0, NMAT), jax.random.fold_in(key_of[2], 1), 0, NMAT - 1).astype(jnp.int32)
    mat_coef = jnp.clip(jnp.exp(jax.random.uniform(key_of[3], (NMAT,), jnp.float32, math.log(0.5), math.log(4.0))), 0.5, 4.0)
    owner_perm = jax.random.permutation(key_of[4], SECTORS).astype(jnp.int32)
    blocks = gaussian(key_of[5], (SECTORS, ORDER, ORDER), ORDER ** -0.5, 0.0625, ((0, 16), (2, 16)))
    return {"rhs": rhs, "flux_in": flux_in, "materials": materials, "mat_coef": mat_coef, "owner_perm": owner_perm, "blocks": blocks}


center = 1.0
radius = 0.93

def harmonic_basis(harmonic_ids, sector_ids, sector_count):
    midpoint = sector_count // 2
    wavenum = jnp.where(harmonic_ids <= midpoint, harmonic_ids, harmonic_ids - midpoint)
    phases = 2.0 * jnp.pi * (wavenum * sector_ids % sector_count).astype(jnp.float32) / sector_count
    basis_value = jnp.where(harmonic_ids <= midpoint, jnp.cos(phases), jnp.sin(phases))
    endpoint = (harmonic_ids == 0) | (harmonic_ids == midpoint)
    weight_scale = jnp.where(endpoint, math.sqrt(1.0 / sector_count), math.sqrt(2.0 / sector_count))
    return (basis_value * weight_scale).astype(jnp.float32)

def neighbour_total(values):
    depth_pad = jnp.pad(values, ((0, 0), (1, 1), (0, 0), (0, 0)))
    total = depth_pad[:, 2:] + depth_pad[:, :-2]
    total = total + jnp.roll(values, 1, 2) + jnp.roll(values, -1, 2)
    total = total + jnp.roll(values, 1, 3) + jnp.roll(values, -1, 3)
    return total

def apply_block(operands):
    vector, matrix = operands
    return jnp.dot(vector.astype(jnp.float32), matrix.astype(jnp.float32), preferred_element_type=jnp.float32)

def reference(rhs, flux_in, materials, mat_coef, owner_perm, blocks):
    onehot = (materials[..., None] == jnp.arange(NMAT, dtype=jnp.int32)).astype(jnp.float32)
    sigma = lax.optimization_barrier(jnp.sum(onehot * mat_coef, -1))
    diagonal = 6.0 + sigma
    inverse = 1.0 / diagonal
    source = rhs.at[:, DEPTH - 1].add(flux_in)
    sigma_one = center / radius
    solution = jnp.zeros_like(rhs)
    remainder = source
    direction = remainder * inverse / center
    ratio_now = 1.0 / sigma_one
    for sweep in range(SWEEPS):
        solution = solution + direction
        if sweep + 1 < SWEEPS:
            remainder = remainder - (diagonal * direction - neighbour_total(direction))
            ratio_next = 1.0 / (2.0 * sigma_one - ratio_now)
            direction = ratio_next * ratio_now * direction + 2.0 * ratio_next / radius * remainder * inverse
            ratio_now = ratio_next
    traces = solution[:, DEPTH - 1].astype(jnp.bfloat16).reshape(EXC, NZ, SECTORS, PTS).astype(jnp.float32)
    basis = harmonic_basis(owner_perm[:, None], jnp.arange(SECTORS, dtype=jnp.int32)[None, :], SECTORS)
    harmonics = jnp.einsum('ds,ezsp->dezp', basis, traces, precision=lax.Precision.HIGHEST)
    harmonics = harmonics.reshape(SECTORS, EXC, ORDER).astype(jnp.bfloat16)
    response = lax.map(apply_block, (harmonics, blocks))
    response = response.reshape(SECTORS, EXC, NZ, PTS)
    flux_out = jnp.einsum('ds,dezp->ezsp', basis, response, precision=lax.Precision.HIGHEST)
    return (solution, flux_out.reshape(EXC, NZ, SECTORS * PTS))
```

```python
import math

import jax
import jax.numpy as jnp
from jax import lax
from jax.experimental import pallas as pl
from jax.experimental.pallas import tpu as pltpu
from jax.sharding import PartitionSpec as P

SWEEPS = 4
DEEP = SWEEPS - 1

center = 1.0
radius = 0.93

F32 = jnp.float32
BF16 = jnp.bfloat16
ANY = pl.BlockSpec(memory_space=pl.ANY)
SMEM = pl.BlockSpec(memory_space=pltpu.SMEM)
VMEM = pl.BlockSpec(memory_space=pltpu.VMEM)

EXC, DEPTH, ROWS, PTS, PARTS = 64, 8, 4, 128, 16
CELLS = DEPTH * ROWS
EDGE = EXC + 16
BULK = DEPTH * DEEP * EXC
SLAB = BULK + 32 + 2 * EDGE
GROUP = 16
WIDE = ROWS + 2 * DEEP


def harmonic_basis(harmonic_ids, sector_ids, sector_count):
    midpoint = sector_count // 2
    wavenum = jnp.where(harmonic_ids <= midpoint, harmonic_ids, harmonic_ids - midpoint)
    phases = 2.0 * jnp.pi * (wavenum * sector_ids % sector_count).astype(F32) / sector_count
    basis_value = jnp.where(harmonic_ids <= midpoint, jnp.cos(phases), jnp.sin(phases))
    endpoint = (harmonic_ids == 0) | (harmonic_ids == midpoint)
    weight_scale = jnp.where(endpoint, math.sqrt(1.0 / sector_count), math.sqrt(2.0 / sector_count))
    return basis_value * weight_scale


def lanes_of(shape):
    return lax.broadcasted_iota(jnp.int32, shape, len(shape) - 1)


def source_row(rhs_ref, flux_ref, cell, start, count):
    row = rhs_ref[pl.ds(start * CELLS + cell, count, stride=CELLS), :]
    if cell // ROWS == DEPTH - 1:
        row = row + flux_ref[pl.ds(start * ROWS + cell % ROWS, count, stride=ROWS), :]
    return row


def edge_kernel(rhs_ref, flux_ref, mat_ref, low_ref, high_ref):
    slot = lanes_of((EXC, PTS)) // 4
    low = high = jnp.zeros((EXC, PTS), F32)
    for cell in range(CELLS):
        row = source_row(rhs_ref, flux_ref, cell, 0, EXC)
        low = jnp.where(slot == cell, pltpu.roll(row, 4 * cell, 1) if cell else row, low)
        high = jnp.where(slot == cell, pltpu.roll(row, (4 * cell + 4) % PTS, 1) if cell < 31 else row, high)
    slot = lanes_of((1, PTS)) // 4
    mlow = mhigh = jnp.zeros((1, PTS), F32)
    for cell in range(CELLS):
        row = mat_ref[cell : cell + 1, :].astype(F32)
        mlow = jnp.where(slot == cell, pltpu.roll(row, 4 * cell, 1) if cell else row, mlow)
        mhigh = jnp.where(slot == cell, pltpu.roll(row, (4 * cell + 4) % PTS, 1) if cell < 31 else row, mhigh)
    low_ref[0:EXC, :] = low.astype(BF16)
    high_ref[0:EXC, :] = high.astype(BF16)
    low_ref[EXC:EDGE, :] = jnp.broadcast_to(mlow, (16, PTS)).astype(BF16)
    high_ref[EXC:EDGE, :] = jnp.broadcast_to(mhigh, (16, PTS)).astype(BF16)


def slab_kernel(rhs_ref, flux_ref, mat_ref, top_ref, bot_ref):
    mtop, mbot = [], []
    for d in range(DEPTH):
        for z in range(ROWS):
            cell = d * ROWS + z
            row = source_row(rhs_ref, flux_ref, cell, 0, EXC).astype(BF16)
            if z < DEEP:
                top_ref[pl.ds((d * DEEP + z) * EXC, EXC), :] = row
            if z >= ROWS - DEEP:
                bot_ref[pl.ds((d * DEEP + z - ROWS + DEEP) * EXC, EXC), :] = row
        mtop.append(mat_ref[d * ROWS : d * ROWS + DEEP, :].astype(F32))
        mbot.append(mat_ref[d * ROWS + ROWS - DEEP : (d + 1) * ROWS, :].astype(F32))
    pad = [jnp.zeros((32 - DEPTH * DEEP, PTS), F32)]
    top_ref[BULK : BULK + 32, :] = jnp.concatenate(mtop + pad, 0).astype(BF16)
    bot_ref[BULK : BULK + 32, :] = jnp.concatenate(mbot + pad, 0).astype(BF16)


def unpack(right, left, cell):
    a = pltpu.roll(right, PTS - 4 * cell, 1) if cell else right
    b = pltpu.roll(left, PTS - 4 - 4 * cell, 1) if cell < 31 else left
    return jnp.where(lanes_of(a.shape) < PTS // 2, a, b)


def sweep_kernel(coef_ref, rhs_ref, flux_ref, mat_ref, right_ref, left_ref, next_ref, prev_ref,
                 sol_ref, tr_ref, dg_ref, iv_ref, r_ref, p0_ref, p1_ref, p2_ref, trf_ref):
    def pieces(z):
        if z < DEEP:
            return prev_ref, z, z + ROWS - DEEP
        if z >= DEEP + ROWS:
            return next_ref, z - DEEP - ROWS, z - DEEP - ROWS
        return None, None, z - DEEP

    def edges(slab):
        if slab is None:
            return right_ref, left_ref, 0, 0
        return slab, slab, BULK + 32, BULK + 32 + EDGE

    for d in range(DEPTH):
        rows = []
        for z in range(WIDE):
            slab, k, own = pieces(z)
            cell = d * ROWS + own
            if slab is None:
                mid = mat_ref[cell : cell + 1, :].astype(F32)
            else:
                base = BULK + (d * DEEP + k) // 16 * 16
                off = (d * DEEP + k) % 16
                mid = slab[base : base + 16, :].astype(F32)[off : off + 1, :]
            ra, la, ro, lo = edges(slab)
            right = ra[ro + EXC : ro + EDGE, :].astype(F32)[0:1, :]
            left = la[lo + EXC : lo + EDGE, :].astype(F32)[0:1, :]
            rows.append(jnp.concatenate([mid, unpack(right, left, cell)], 1))
        mat = jnp.concatenate(rows, 0)
        sigma = jnp.zeros(mat.shape, F32)
        for m in range(8):
            sigma = jnp.where(mat == float(m), coef_ref[m], sigma)
        diagonal = 6.0 + sigma
        inverse = 1.0 / diagonal
        for z in range(WIDE):
            dg_ref[d, z] = jnp.broadcast_to(diagonal[z : z + 1], (8, 2 * PTS))
            iv_ref[d, z] = jnp.broadcast_to(inverse[z : z + 1], (8, 2 * PTS))

    zero = jnp.zeros((GROUP, 2 * PTS), F32)
    for ref in (p0_ref, p1_ref, p2_ref):
        for z in range(WIDE):
            ref[0, z] = zero
            ref[DEPTH + 1, z] = zero

    def both(v):
        return jnp.concatenate([v, v], 0)

    def one_group(g, carry):
        at = pl.multiple_of(g * GROUP, GROUP)
        for d in range(DEPTH):
            for z in range(WIDE):
                slab, k, own = pieces(z)
                cell = d * ROWS + own
                if slab is None:
                    mid = source_row(rhs_ref, flux_ref, cell, at, GROUP)
                else:
                    mid = slab[pl.ds((d * DEEP + k) * EXC + at, GROUP), :].astype(F32)
                ra, la, ro, lo = edges(slab)
                right = ra[pl.ds(ro + at, GROUP), :].astype(F32)
                left = la[pl.ds(lo + at, GROUP), :].astype(F32)
                row = jnp.concatenate([mid, unpack(right, left, cell)], 1)
                r_ref[d, z] = row
                p0_ref[d + 1, z] = row * both(iv_ref[d, z]) / center
        sigma_one = center / radius
        ratio_now = 1.0 / sigma_one
        bufs = (p0_ref, p1_ref, p2_ref)
        for sweep in range(DEEP):
            ratio_next = 1.0 / (2.0 * sigma_one - ratio_now)
            keep, step = ratio_next * ratio_now, 2.0 * ratio_next / radius
            p, last = bufs[sweep], sweep + 1 == DEEP

            def layer(d, carry, p=p, last=last, sweep=sweep, keep=keep, step=step):
                for z in range(1 + sweep, WIDE - 1 - sweep):
                    c = p[d + 1, z]
                    total = p[d, z] + p[d + 2, z]
                    total = total + (p[d + 1, z + 1] + p[d + 1, z - 1])
                    total = total + (pltpu.roll(c, 1, 1) + pltpu.roll(c, 2 * PTS - 1, 1))
                    r = r_ref[d, z] - (both(dg_ref[d, z]) * c - total)
                    new = keep * c + step * (r * both(iv_ref[d, z]))
                    if last:
                        out = ((p0_ref[d + 1, z] + p1_ref[d + 1, z]) + c + new)[:, :PTS]
                        own = z - DEEP
                        sol_ref[pl.ds(at * CELLS + d * ROWS + own, GROUP, stride=CELLS), :] = out
                        trf_ref[pl.ds(at * ROWS + own, GROUP, stride=ROWS), :] = out
                    else:
                        r_ref[d, z] = r
                        bufs[sweep + 1][d + 1, z] = new
                return carry

            lax.fori_loop(0, DEPTH, layer, 0)
            ratio_now = ratio_next
        return carry

    lax.fori_loop(0, EXC // GROUP, one_group, 0)
    tr_ref[...] = trf_ref[...].astype(BF16)


def transform_kernel(m_ref, x_ref, o_ref, f_ref):
    f_ref[...] = x_ref[...].astype(F32)
    x = jnp.concatenate([f_ref[pl.ds(r, PARTS, stride=PARTS), :] for r in range(PARTS)], 1)
    y = jnp.dot(m_ref[...], x, precision=lax.Precision.HIGHEST, preferred_element_type=F32)
    for r in range(PARTS):
        f_ref[pl.ds(r, PARTS, stride=PARTS), :] = y[:, r * PTS : (r + 1) * PTS]
    o_ref[...] = f_ref[...].astype(BF16)


def block_kernel(idx_ref, mine_ref, peer_ref, w_ref, o_ref, wb_ref, f_ref, sem):
    deep = ROWS * PTS

    def fetch(k):
        return pltpu.make_async_copy(
            w_ref.at[0, pl.ds(pl.multiple_of(idx_ref[k] * deep, deep), deep), :],
            wb_ref.at[pl.ds(k * deep, deep), :], sem.at[k])

    for k in range(16):
        fetch(k).start()
    acc = jnp.zeros((EXC, 512), F32)
    for k in range(16):
        x = (mine_ref if k < 8 else peer_ref)[k % 8]
        f_ref[pl.ds(k * 256, 256), :] = x.astype(F32)
        x = jnp.concatenate([f_ref[pl.ds(k * 256 + z, EXC, stride=ROWS), :] for z in range(ROWS)], 1)
        fetch(k).wait()
        acc = acc + jnp.dot(x.astype(BF16), wb_ref[pl.ds(k * deep, deep), :], preferred_element_type=F32)
    for z in range(ROWS):
        f_ref[pl.ds(z, EXC, stride=ROWS), :] = acc[:, z * PTS : (z + 1) * PTS]
    o_ref[...] = f_ref[0:256, :].astype(BF16)


def vol_move(x, dest):
    pairs = []
    for i in range(16):
        zh, y, c = dest(i // 8, i // 2 % 4, i % 2)
        pairs.append((i, zh % 2 * 8 + y % 4 * 2 + c % 2))
    return lax.ppermute(x, "vol", pairs)


def gather_vol(x):
    pair = jnp.stack([x, vol_move(x, lambda zh, y, c: (zh + 1, y, c))])
    mine = jnp.concatenate([pair] + [vol_move(pair, lambda zh, y, c, k=k: (zh, y + k, c)) for k in (1, 3, 2)])
    peer = vol_move(mine, lambda zh, y, c: (zh, y, c + 1))
    me = lax.axis_index("vol")
    zh, y, c = me // 8, me // 2 % 4, me % 2
    own = [(zh + a) % 2 * 8 + (y - k) % 4 * 2 for k in (0, 1, 3, 2) for a in (0, 1)]
    index = jnp.stack([v + c for v in own] + [v + 1 - c for v in own])
    return mine, peer, index.astype(jnp.int32)


def exchange(x):
    return lax.all_to_all(x.reshape(PARTS, 16, PTS), "sec", 0, 0, tiled=True).reshape(256, PTS)


def per_device(rhs, flux_in, materials, mat_coef, owner_perm, blocks):
    shape = jax.ShapeDtypeStruct
    rhs2 = rhs.reshape(EXC * CELLS, PTS)
    flux2 = flux_in.reshape(EXC * ROWS, PTS)
    mat2 = materials.reshape(CELLS, PTS)
    ring = [(i, (i + 1) % 16) for i in range(16)]
    back = [((i + 1) % 16, i) for i in range(16)]

    low, high = pl.pallas_call(
        edge_kernel, out_shape=(shape((EDGE, PTS), BF16),) * 2, in_specs=[VMEM] * 3, out_specs=(VMEM,) * 2, name="edges",
    )(rhs2, flux2, mat2)
    right = lax.ppermute(low, "sec", back)
    left = lax.ppermute(high, "sec", ring)
    top, bot = pl.pallas_call(
        slab_kernel, out_shape=(shape((SLAB, PTS), BF16),) * 2, in_specs=[VMEM] * 3, out_specs=(VMEM,) * 2, name="slabs",
    )(rhs2, flux2, mat2)
    sides = jnp.concatenate([right, left])
    top = lax.dynamic_update_slice(top, sides, (BULK + 32, 0))
    bot = lax.dynamic_update_slice(bot, sides, (BULK + 32, 0))
    nxt = lax.ppermute(top, "vol", back)
    prev = lax.ppermute(bot, "vol", ring)

    field = pltpu.VMEM((DEPTH + 2, WIDE, GROUP, 2 * PTS), F32)
    solution, traces = pl.pallas_call(
        sweep_kernel,
        out_shape=(shape((EXC * CELLS, PTS), F32), shape((EXC * ROWS, PTS), BF16)),
        in_specs=[SMEM] + [VMEM] * 7, out_specs=(VMEM,) * 2,
        scratch_shapes=[pltpu.VMEM((DEPTH, WIDE, 8, 2 * PTS), F32)] * 2
        + [pltpu.VMEM((DEPTH, WIDE, GROUP, 2 * PTS), F32)] + [field] * 3 + [pltpu.VMEM((EXC * ROWS, PTS), F32)],
        name="sweeps",
    )(mat_coef, rhs2, flux2, mat2, right, left, nxt, prev)

    basis = harmonic_basis(owner_perm[:, None], jnp.arange(PARTS, dtype=jnp.int32)[None, :], PARTS)

    def transform(matrix, x):
        return pl.pallas_call(
            transform_kernel, out_shape=shape((256, PTS), BF16), in_specs=[VMEM] * 2, out_specs=VMEM,
            scratch_shapes=[pltpu.VMEM((256, PTS), F32)], name="transform",
        )(matrix, x)

    harmonics = exchange(transform(basis, exchange(traces)))
    mine, peer, index = gather_vol(harmonics)
    response = pl.pallas_call(
        block_kernel, out_shape=shape((256, PTS), BF16), in_specs=[SMEM, VMEM, VMEM, ANY], out_specs=VMEM,
        scratch_shapes=[pltpu.VMEM((8192, 512), BF16), pltpu.VMEM((4096, PTS), F32), pltpu.SemaphoreType.DMA((16,))],
        name="block",
    )(index, mine.reshape(8, 256, PTS), peer.reshape(8, 256, PTS), blocks)
    flux = exchange(transform(basis.T, exchange(response)))
    return solution.reshape(EXC, DEPTH, ROWS, PTS), flux.astype(F32).reshape(EXC, ROWS, PTS)


def solution(mesh):
    return jax.shard_map(
        per_device,
        mesh=mesh,
        in_specs=(
            P(None, None, "vol", "sec"),
            P(None, "vol", "sec"),
            P(None, "vol", "sec"),
            P(),
            P(),
            P("sec", None, "vol"),
        ),
        out_specs=(P(None, None, "vol", "sec"), P(None, "vol", "sec")),
        check_vma=False,
    )
```

```python
import math

import jax
import jax.numpy as jnp
from jax import lax
from jax.experimental import pallas as pl
from jax.experimental.pallas import tpu as pltpu
from jax.sharding import PartitionSpec as P

SWEEPS = 4
DEEP = SWEEPS - 1

center = 1.0
radius = 0.93

F32 = jnp.float32
BF16 = jnp.bfloat16
SMEM = pl.BlockSpec(memory_space=pltpu.SMEM)
VMEM = pl.BlockSpec(memory_space=pltpu.VMEM)
HBM = pl.BlockSpec(memory_space=pltpu.HBM)

EXC, DEPTH, ROWS, PTS, PARTS = 64, 8, 4, 128, 16
CELLS = DEPTH * ROWS
EDGE = EXC + 16
BULK = DEPTH * DEEP * EXC
SLAB = BULK + 32 + 2 * EDGE
GROUP = 16
WIDE = ROWS + 2 * DEEP
TALL = SWEEPS * ROWS
MINE = EXC // PARTS
PIECE = TALL * (MINE + 1)
RIM = [(d, k) for d in range(SWEEPS - 1, 0, -1) for k in range(d)]

VOL = ("zh", "y", "c")
SEC = ("zl", "x")


def basis_of(perm_ref, by_sector):
    shape = (PARTS, PARTS)
    own = lax.broadcasted_iota(jnp.int32, shape, 1 if by_sector else 0)
    sector = lax.broadcasted_iota(jnp.int32, shape, 0 if by_sector else 1)
    ids = jnp.zeros(shape, jnp.int32)
    for d in range(PARTS):
        ids = jnp.where(own == d, perm_ref[d], ids)
    half, quarter = PARTS // 2, PARTS // 4
    even = ids <= half
    turn = jnp.where(even, ids, ids - half) * sector
    turn = (turn + jnp.where(even, 0, PARTS - quarter)) & (PARTS - 1)
    value = jnp.zeros(shape, F32)
    for n in range(PARTS):
        value = jnp.where(turn == n, math.cos(2.0 * math.pi * n / PARTS) if n % half != quarter else 0.0, value)
    ends = (ids == 0) | (ids == half)
    return value * jnp.where(ends, math.sqrt(1.0 / PARTS), math.sqrt(2.0 / PARTS))


def lanes_of(shape):
    return lax.broadcasted_iota(jnp.int32, shape, len(shape) - 1)


def source_row(rhs_ref, flux_ref, cell, start, count):
    row = rhs_ref[pl.ds(start * CELLS + cell, count, stride=CELLS), :]
    if cell // ROWS == DEPTH - 1:
        row = row + flux_ref[pl.ds(start * ROWS + cell % ROWS, count, stride=ROWS), :]
    return row


def sigma_of(table_ref, mat):
    sigma = jnp.zeros(mat.shape, F32)
    for m in range(8):
        sigma = jnp.where(mat == float(m), table_ref[m : m + 1, :], sigma)
    return sigma


def by_core(first, second):
    core = lax.axis_index("c")
    pl.when(core == 0)(first)
    pl.when(core == 1)(second)


def share_kernel(rhs_hbm, flux_hbm, mat_hbm, o_ref, rhs_ref, flux_ref, mat_ref, sem):
    copies = [
        pltpu.make_async_copy(rhs_hbm.at[:, pl.ds(CELLS - TALL, TALL), :], rhs_ref, sem.at[0]),
        pltpu.make_async_copy(flux_hbm, flux_ref, sem.at[1]),
        pltpu.make_async_copy(mat_hbm, mat_ref, sem.at[2]),
    ]
    for copy in copies:
        copy.start()
    for copy in copies:
        copy.wait()
    mat = mat_ref[CELLS - TALL : CELLS, :].astype(F32).astype(BF16)
    for e in range(EXC):
        k, own = e // MINE, e % MINE
        f = jnp.concatenate([jnp.zeros((TALL - ROWS, PTS), F32), flux_ref[e * ROWS : (e + 1) * ROWS, :]], 0)
        o_ref[k * PIECE + own * TALL : k * PIECE + (own + 1) * TALL, :] = (rhs_ref[e] + f).astype(BF16)
        if own == 0:
            o_ref[k * PIECE + MINE * TALL : (k + 1) * PIECE, :] = mat


def rim_kernel(x_ref, o_ref, near_ref, far_ref, f_ref):
    f_ref[...] = x_ref[...].astype(F32)
    for r in range(PIECE):
        o_ref[r * PARTS : (r + 1) * PARTS, :] = f_ref[pl.ds(r, PARTS, stride=PIECE), :].astype(BF16)

    def fill(top_ref, bot_ref):
        at = 0
        for d, k in RIM:
            for own in range(MINE + 1):
                top, bot = own * TALL + d * ROWS + k, own * TALL + d * ROWS + ROWS - 1 - k
                top_ref[at : at + PARTS, :] = o_ref[top * PARTS : (top + 1) * PARTS, :]
                bot_ref[at : at + PARTS, :] = o_ref[bot * PARTS : (bot + 1) * PARTS, :]
                at += PARTS

    by_core(lambda: fill(far_ref, near_ref), lambda: fill(near_ref, far_ref))


def take_sides(near_ref, far_ref, next_ref, prev_ref):
    def take(a, b):
        next_ref[...] = a[...]
        prev_ref[...] = b[...]

    by_core(lambda: take(near_ref, far_ref), lambda: take(far_ref, near_ref))


def trace_kernel(table_ref, x_ref, near_ref, far_ref, o_ref, f_ref, next_ref, prev_ref):
    take_sides(near_ref, far_ref, next_ref, prev_ref)

    def tile(own, d, z):
        if 0 <= z < ROWS:
            ref, at = x_ref, own * TALL + d * ROWS + z
        else:
            ref, k = (prev_ref, -1 - z) if z < 0 else (next_ref, z - ROWS)
            at = RIM.index((d, k)) * (MINE + 1) + own
        return ref[at * PARTS : (at + 1) * PARTS, :].astype(F32)

    top = SWEEPS - 1
    diagonal, inverse = {}, {}
    for d in range(SWEEPS):
        for z in range(-d, ROWS + d):
            diagonal[d, z] = 6.0 + sigma_of(table_ref, tile(MINE, d, z))
            inverse[d, z] = 1.0 / diagonal[d, z]
    lane = lanes_of((PARTS, PTS))

    def sides(v):
        a, b = pltpu.roll(v, 1, 1), pltpu.roll(v, PTS - 1, 1)
        a = jnp.where(lane == 0, pltpu.roll(a, 1, 0), a)
        b = jnp.where(lane == PTS - 1, pltpu.roll(b, PARTS - 1, 0), b)
        return a + b

    sigma_one = center / radius
    traces = []
    for own in range(MINE):
        r = {at: tile(own, *at) for at in diagonal}
        p = {at: r[at] * inverse[at] / center for at in diagonal}
        total = {z: p[top, z] for z in range(ROWS)}
        ratio_now = 1.0 / sigma_one
        for sweep in range(DEEP):
            ratio_next = 1.0 / (2.0 * sigma_one - ratio_now)
            keep, step = ratio_next * ratio_now, 2.0 * ratio_next / radius
            new = {}
            for d in range(sweep + 1, SWEEPS):
                reach = d - sweep - 1
                for z in range(-reach, ROWS + reach):
                    near = p[d - 1, z] + (p[d, z - 1] + p[d, z + 1]) + sides(p[d, z])
                    if d < top:
                        near = near + p[d + 1, z]
                    r[d, z] = r[d, z] - (diagonal[d, z] * p[d, z] - near)
                    new[d, z] = keep * p[d, z] + step * (r[d, z] * inverse[d, z])
            p, ratio_now = new, ratio_next
            total = {z: total[z] + p[top, z] for z in range(ROWS)}
        traces += [total[z].astype(BF16).astype(F32) for z in range(ROWS)]
    y = jnp.dot(table_ref[8:24, :PARTS], jnp.concatenate(traces, 1),
                precision=lax.Precision.HIGHEST, preferred_element_type=F32)
    for k in range(MINE * ROWS):
        f_ref[pl.ds(k, PARTS, stride=MINE * ROWS), :] = y[:, k * PTS : (k + 1) * PTS]
    out = f_ref[...].astype(BF16)
    o_ref[0:256, :] = out
    o_ref[256:512, :] = out


def roll(x, lanes):
    lanes %= PTS
    return pltpu.roll(x, lanes, 1) if lanes else x


def pack_edges(row, cell, low, high):
    lane = lanes_of(row.shape)
    for j in range(DEEP):
        low = jnp.where(lane == 4 * cell + 3 - j, roll(row, 4 * cell + 3 - 2 * j), low)
        high = jnp.where(lane == 4 * cell + j, roll(row, 4 * cell + 2 * j + 1), high)
    return low, high


def edge_kernel(coef_hbm, perm_hbm, rhs_hbm, flux_hbm, mat_hbm, low_ref, high_ref, near_ref, far_ref, table_ref,
                coef_ref, perm_ref, rhs_ref, flux_ref, mat_ref, sem):
    pairs = ((rhs_hbm, rhs_ref), (flux_hbm, flux_ref), (mat_hbm, mat_ref), (coef_hbm, coef_ref), (perm_hbm, perm_ref))
    copies = [pltpu.make_async_copy(*pair, sem.at[k]) for k, pair in enumerate(pairs)]
    for copy in copies:
        copy.start()
    for copy in copies:
        copy.wait()
    by_core(lambda: fill_slabs(rhs_ref, flux_ref, mat_ref, far_ref, near_ref),
            lambda: fill_slabs(rhs_ref, flux_ref, mat_ref, near_ref, far_ref))
    for m in range(8):
        table_ref[m : m + 1, :] = jnp.full((1, PTS), coef_ref[m], F32)
    for at, by_sector in ((8, False), (24, True)):
        table_ref[at : at + PARTS, :PARTS] = basis_of(perm_ref, by_sector)
    sides = (jnp.zeros((EXC, PTS), F32),) * 2
    mats = (jnp.zeros((1, PTS), F32),) * 2
    for cell in range(CELLS):
        sides = pack_edges(source_row(rhs_ref, flux_ref, cell, 0, EXC), cell, *sides)
        mats = pack_edges(mat_ref[cell : cell + 1, :].astype(F32), cell, *mats)
    for ref, side, mat in zip((low_ref, high_ref), sides, mats):
        ref[0:EXC, :] = side.astype(BF16)
        ref[EXC:EDGE, :] = jnp.broadcast_to(mat, (16, PTS)).astype(BF16)


def fill_slabs(rhs_ref, flux_ref, mat_ref, top_ref, bot_ref):
    mtop, mbot = [], []
    for d in range(DEPTH):
        for z in range(ROWS):
            cell = d * ROWS + z
            row = source_row(rhs_ref, flux_ref, cell, 0, EXC).astype(BF16)
            if z < DEEP:
                top_ref[pl.ds((d * DEEP + z) * EXC, EXC), :] = row
            if z >= ROWS - DEEP:
                bot_ref[pl.ds((d * DEEP + z - ROWS + DEEP) * EXC, EXC), :] = row
        mtop.append(mat_ref[d * ROWS : d * ROWS + DEEP, :].astype(F32))
        mbot.append(mat_ref[d * ROWS + ROWS - DEEP : (d + 1) * ROWS, :].astype(F32))
    pad = [jnp.zeros((32 - DEPTH * DEEP, PTS), F32)]
    top_ref[BULK : BULK + 32, :] = jnp.concatenate(mtop + pad, 0).astype(BF16)
    bot_ref[BULK : BULK + 32, :] = jnp.concatenate(mbot + pad, 0).astype(BF16)


def place_edges(halo, right, left, cell, z):
    lane = lanes_of(halo.shape)
    both = jnp.where(lane % 8 < 4, roll(right, 8 * z - 4 * cell), roll(left, 8 * z + 4 - 4 * cell))
    return jnp.where(lane // 8 == z, both, halo)


def sweep_kernel(half, table_ref, rhs_ref, flux_ref, mat_ref, right_ref, left_ref, near_ref, far_ref, *refs):
    (out_hbm, dg_ref, iv_ref, r_ref, p0_ref, p1_ref, p2_ref, dgh_ref, ivh_ref, rh_ref, h0_ref, h1_ref, h2_ref,
     next_ref, prev_ref, sol_ref, sem) = refs[half:]
    take_sides(near_ref, far_ref, next_ref, prev_ref)

    def where_is(z):
        if z < DEEP:
            return prev_ref, z, z + ROWS - DEEP
        if z >= DEEP + ROWS:
            return next_ref, z - DEEP - ROWS, z - DEEP - ROWS
        return None, None, z - DEEP

    def edges(slab, at, count):
        if slab is None:
            return [ref[pl.ds(at, count), :].astype(F32) for ref in (right_ref, left_ref)]
        return [slab[pl.ds(BULK + 32 + off + at, count), :].astype(F32) for off in (0, EDGE)]

    for d in range(DEPTH):
        halo = jnp.zeros((16, PTS), F32)
        for z in range(WIDE):
            slab, k, own = where_is(z)
            cell = d * ROWS + own
            if slab is None:
                mid = mat_ref[cell : cell + 1, :].astype(F32)
            else:
                base, off = BULK + (d * DEEP + k) // 16 * 16, (d * DEEP + k) % 16
                mid = slab[base : base + 16, :].astype(F32)[off : off + 1, :]
            diagonal = 6.0 + sigma_of(table_ref, mid)
            dg_ref[d, z] = jnp.broadcast_to(diagonal, (8, PTS))
            iv_ref[d, z] = jnp.broadcast_to(1.0 / diagonal, (8, PTS))
            halo = place_edges(halo, *edges(slab, EXC, 16), cell, z)
        diagonal = 6.0 + sigma_of(table_ref, halo[0:8])
        dgh_ref[d] = diagonal
        ivh_ref[d] = 1.0 / diagonal

    zero = jnp.zeros((GROUP, PTS), F32)
    fields, halos = (p0_ref, p1_ref, p2_ref), (h0_ref, h1_ref, h2_ref)
    for field, halo in zip(fields, halos):
        for d in (0, DEPTH + 1):
            halo[d] = zero
            for z in range(WIDE):
                field[d, z] = zero

    def both(v):
        return jnp.concatenate([v, v], 0)

    lane = lanes_of((GROUP, PTS))
    spot = lane % 8

    def send(g):
        rows = GROUP * CELLS
        return pltpu.make_async_copy(
            sol_ref.at[pl.ds(pl.multiple_of(g * rows, rows), rows), :],
            out_hbm.at[pl.ds(pl.multiple_of(half * EXC // 2 * CELLS + g * rows, rows), rows), :], sem.at[g])

    def one_group(g, carry):
        at = pl.multiple_of(half * EXC // 2 + g * GROUP, GROUP)
        packed = {id(slab): edges(slab, at, GROUP) for slab in (None, next_ref, prev_ref)}
        for d in range(DEPTH):
            halo = zero
            for z in range(WIDE):
                slab, k, own = where_is(z)
                cell = d * ROWS + own
                if slab is None:
                    mid = source_row(rhs_ref, flux_ref, cell, at, GROUP)
                else:
                    mid = slab[pl.ds((d * DEEP + k) * EXC + at, GROUP), :].astype(F32)
                halo = place_edges(halo, *packed[id(slab)], cell, z)
                r_ref[d, z] = mid
                p0_ref[d + 1, z] = mid * both(iv_ref[d, z]) / center
            rh_ref[d] = halo
            h0_ref[d + 1] = halo * both(ivh_ref[d]) / center
        sigma_one = center / radius
        ratio_now = 1.0 / sigma_one
        for sweep in range(DEEP):
            ratio_next = 1.0 / (2.0 * sigma_one - ratio_now)
            keep, step = ratio_next * ratio_now, 2.0 * ratio_next / radius
            last = sweep + 1 == DEEP

            def layer(d, carry, p=fields[sweep], h=halos[sweep], last=last, sweep=sweep, keep=keep, step=step):
                side = h[d + 1]
                ends = zero
                for z in range(1 + sweep, WIDE - 1 - sweep):
                    c = p[d + 1, z]
                    beside = roll(side, -8 * z - 4)
                    total = p[d, z] + p[d + 2, z]
                    total = total + (p[d + 1, z + 1] + p[d + 1, z - 1])
                    total = total + (jnp.where(lane == 0, beside, roll(c, 1)) + jnp.where(lane == PTS - 1, beside, roll(c, -1)))
                    r = r_ref[d, z] - (both(dg_ref[d, z]) * c - total)
                    new = keep * c + step * (r * both(iv_ref[d, z]))
                    if last:
                        out = (p0_ref[d + 1, z] + p1_ref[d + 1, z]) + c + new
                        sol_ref[pl.ds(g * GROUP * CELLS + d * ROWS + z - DEEP, GROUP, stride=CELLS), :] = out
                    else:
                        r_ref[d, z] = r
                        fields[sweep + 1][d + 1, z] = new
                        ends = jnp.where((lane == 8 * z + 3) | (lane == 8 * z + 4), roll(c, 8 * z + 4), ends)
                if not last:
                    total = h[d] + h[d + 2] + (roll(side, 8) + roll(side, -8)) + ends
                    total = total + (jnp.where(spot == 4, 0.0, roll(side, 1)) + jnp.where(spot == 3, 0.0, roll(side, -1)))
                    r = rh_ref[d] - (both(dgh_ref[d]) * side - total)
                    rh_ref[d] = r
                    halos[sweep + 1][d + 1] = keep * side + step * (r * both(ivh_ref[d]))
                return carry

            lax.fori_loop(0, DEPTH, layer, 0, unroll=2)
            ratio_now = ratio_next
        send(g).start()
        return carry

    count = EXC // GROUP // 2
    lax.fori_loop(0, count, one_group, 0)
    for g in range(count):
        send(g).wait()


def gate_kernel(x_ref, o_ref):
    o_ref[...] = x_ref[...]


def flux_kernel(table_ref, x_ref, o_ref, f_ref):
    f_ref[...] = x_ref[...].astype(F32)
    x = jnp.concatenate([f_ref[pl.ds(r, PARTS, stride=PARTS), :] for r in range(PARTS)], 1)
    y = jnp.dot(table_ref[24:40, :PARTS], x, precision=lax.Precision.HIGHEST, preferred_element_type=F32)
    for r in range(PARTS):
        f_ref[pl.ds(r, PARTS, stride=PARTS), :] = y[:, r * PTS : (r + 1) * PTS]
    o_ref[...] = f_ref[...].astype(BF16)


def block_kernel(idx_ref, *refs):
    pieces, (w_ref, o_ref, wb_ref, f_ref, sem) = refs[:8], refs[8:]
    deep = ROWS * PTS

    def fetch(k):
        return pltpu.make_async_copy(
            w_ref.at[0, pl.ds(pl.multiple_of(idx_ref[k] * deep, deep), deep), :],
            wb_ref.at[pl.ds(k * deep, deep), :], sem.at[k])

    for k in range(16):
        fetch(k).start()
    for k in range(16):
        f_ref[pl.ds(k * 256, 256), :] = pieces[k // 2][k % 2].astype(F32)
    acc = jnp.zeros((EXC, 512), F32)
    for k in range(16):
        x = jnp.concatenate([f_ref[pl.ds(k * 256 + z, EXC, stride=ROWS), :] for z in range(ROWS)], 1)
        fetch(k).wait()
        acc = acc + jnp.dot(x.astype(BF16), wb_ref[pl.ds(k * deep, deep), :], preferred_element_type=F32)
    for z in range(ROWS):
        f_ref[pl.ds(z, EXC, stride=ROWS), :] = acc[:, z * PTS : (z + 1) * PTS]
    o_ref[...] = f_ref[0:256, :].astype(BF16)


def shape(rows, dtype=BF16, cols=PTS):
    return jax.ShapeDtypeStruct((rows, cols), dtype)


def call(kernel, out, ins, scratch=(), mib=8, **more):
    outs = out if isinstance(out, tuple) else (out,)
    got = pl.pallas_call(
        kernel, out_shape=outs, in_specs=list(ins), scratch_shapes=list(scratch),
        **({"out_specs": (VMEM,) * len(outs)} | more),
        compiler_params=pltpu.CompilerParams(vmem_limit_bytes=mib << 20))
    return got if isinstance(out, tuple) else (lambda *args: got(*args)[0])


def in_hbm(x):
    return pltpu.with_memory_space_constraint(x, pltpu.HBM)


def exchange(x):
    return lax.all_to_all(x.reshape(PARTS, -1, PTS), SEC, 0, 0, tiled=True).reshape(-1, PTS)


def response_of(pair, blocks):
    y, c = lax.axis_index("y"), lax.axis_index("c")

    def rows(k, core):
        return [a * 8 + (y - k) % 4 * 2 + core for a in (0, 1)]

    def swap(v):
        return lax.ppermute(v, "c", [(0, 1), (1, 0)])

    moved = {k: lax.ppermute(pair, "y", [(i, (i + k) % 4) for i in range(4)]) for k in (1, 3, 2)}
    moved[0] = pair
    pieces, index = [], []
    for k in (0, 1, 3, 2):
        pieces += [moved[k], swap(moved[k])]
        index += rows(k, c) + rows(k, 1 - c)
    return call(
        block_kernel, shape(256), [SMEM] + [VMEM] * 8 + [HBM],
        [pltpu.VMEM((8192, 512), BF16), pltpu.VMEM((16 * 256, PTS), F32), pltpu.SemaphoreType.DMA((16,))], mib=16,
    )(jnp.stack(index).astype(jnp.int32), *pieces, in_hbm(blocks))


def per_device(rhs, flux_in, materials, mat_coef, owner_perm, blocks):
    rhs2 = rhs.reshape(EXC * CELLS, PTS)
    flux2 = flux_in.reshape(EXC * ROWS, PTS)
    mat2 = materials.reshape(CELLS, PTS)
    ring = [(i, (i + 1) % 16) for i in range(16)]
    back = [((i + 1) % 16, i) for i in range(16)]
    tie = lax.optimization_barrier

    def near(x):
        return lax.ppermute(x, VOL, [(i, i ^ 1) for i in range(16)])

    def far(x):
        return lax.ppermute(x, VOL, [(i, (i + 1 if i % 2 else i - 1) % 16) for i in range(16)])

    shared = exchange(call(
        share_kernel, shape(PARTS * PIECE), [HBM] * 3,
        [pltpu.VMEM((EXC, TALL, PTS), F32), pltpu.VMEM((EXC * ROWS, PTS), F32), pltpu.VMEM((CELLS, PTS), jnp.int32),
         pltpu.SemaphoreType.DMA((3,))],
    )(*map(in_hbm, (rhs.reshape(EXC, CELLS, PTS), flux2, mat2))))
    low, high, near_slab, far_slab, table = call(
        edge_kernel, (shape(EDGE), shape(EDGE), shape(SLAB), shape(SLAB), shape(40, F32)), [HBM] * 5,
        [pltpu.SMEM((8,), F32), pltpu.SMEM((PARTS,), jnp.int32), pltpu.VMEM((EXC * CELLS, PTS), F32),
         pltpu.VMEM((EXC * ROWS, PTS), F32), pltpu.VMEM((CELLS, PTS), jnp.int32), pltpu.SemaphoreType.DMA((5,))],
    )(*map(in_hbm, (mat_coef, owner_perm, rhs2, flux2, mat2)))
    right = lax.ppermute(low, SEC, back)
    left = lax.ppermute(high, SEC, ring)
    shared, near_slab, far_slab, table = tie((shared, near_slab, far_slab, table))

    rim = shape(len(RIM) * (MINE + 1) * PARTS)
    own, near_rim, far_rim = call(
        rim_kernel, (shape(PARTS * PIECE), rim, rim), [VMEM], [pltpu.VMEM((PARTS * PIECE, PTS), F32)])(shared)
    far_rim, near_rim = far(far_rim), near(near_rim)
    sides = jnp.concatenate([right, left])
    near_slab = lax.dynamic_update_slice(near_slab, sides, (BULK + 32, 0))
    far_slab = lax.dynamic_update_slice(far_slab, sides, (BULK + 32, 0))
    near_rim, far_rim, near_slab, far_slab = tie((near_rim, far_rim, near_slab, far_slab))
    harmonics = call(
        trace_kernel, shape(512), [VMEM] * 4, [pltpu.VMEM((256, PTS), F32)] + [pltpu.VMEM(rim.shape, BF16)] * 2,
    )(table, own, near_rim, far_rim)
    harmonics, near_slab, far_slab = tie((harmonics, near_slab, far_slab))
    pair = lax.all_to_all(harmonics.reshape(32, 16, PTS), ("zh",) + SEC, 0, 0, tiled=True).reshape(2, 256, PTS)
    near_slab, far_slab = near(near_slab), far(far_slab)
    table = call(gate_kernel, shape(40, F32), [VMEM])(table)
    response = exchange(response_of(pair, blocks))

    wide, tall = (DEPTH, WIDE, GROUP, PTS), (DEPTH + 2, WIDE, GROUP, PTS)
    scratch = [(DEPTH, WIDE, 8, PTS)] * 2 + [wide] + [tall] * 3
    scratch += [(DEPTH, 8, PTS)] * 2 + [(DEPTH, GROUP, PTS)] + [(DEPTH + 2, GROUP, PTS)] * 3
    scratch = [pltpu.VMEM(size, F32) for size in scratch] + [pltpu.VMEM((SLAB, PTS), BF16)] * 2
    scratch += [pltpu.VMEM((EXC // 2 * CELLS, PTS), F32), pltpu.SemaphoreType.DMA((EXC // GROUP // 2,))]

    def sweeps(half, *before):
        return call(
            lambda *refs: sweep_kernel(half, *refs), shape(EXC * CELLS, F32), [VMEM] * 8 + [HBM] * half, scratch,
            mib=16, out_specs=(HBM,), input_output_aliases={8: 0} if half else {},
        )(table, rhs2, flux2, mat2, right, left, near_slab, far_slab, *before)

    solution = sweeps(0)
    response, solution = tie((response, solution))
    flux = exchange(call(flux_kernel, shape(256), [VMEM] * 2, [pltpu.VMEM((256, PTS), F32)])(table, response))
    solution = sweeps(1, solution)
    return solution.reshape(EXC, DEPTH, ROWS, PTS), flux.astype(F32).reshape(EXC, ROWS, PTS)


def solution(mesh):
    fine = jax.sharding.Mesh(mesh.devices.reshape(2, 4, 2, 4, 4), VOL + SEC)
    return jax.shard_map(
        per_device,
        mesh=fine,
        in_specs=(P(None, None, VOL, SEC), P(None, VOL, SEC), P(None, VOL, SEC), P(), P(), P(SEC, None, VOL)),
        out_specs=(P(None, None, VOL, SEC), P(None, VOL, SEC)),
        check_vma=False,
    )
```

```python
import math

import jax
import jax.numpy as jnp
from jax import lax
from jax.experimental import pallas as pl
from jax.experimental.pallas import tpu as pltpu
from jax.sharding import PartitionSpec as P

SWEEPS = 4
DEEP = SWEEPS - 1

center = 1.0
radius = 0.93

F32 = jnp.float32
BF16 = jnp.bfloat16
SMEM = pl.BlockSpec(memory_space=pltpu.SMEM)
VMEM = pl.BlockSpec(memory_space=pltpu.VMEM)
HBM = pl.BlockSpec(memory_space=pltpu.HBM)

EXC, DEPTH, ROWS, PTS, PARTS = 64, 8, 4, 128, 16
CELLS = DEPTH * ROWS
EDGE = EXC + 16
BULK = DEPTH * DEEP * EXC
SLAB = BULK + 32 + 2 * EDGE
GROUP = 16
WIDE = ROWS + 2 * DEEP
TALL = SWEEPS * ROWS
MINE = EXC // PARTS
PIECE = TALL * (MINE + 1)
RIM = [(d, k) for d in range(SWEEPS - 1, 0, -1) for k in range(d)]

VOL = ("zh", "y", "c")
SEC = ("zl", "x")


def basis_of(perm_ref, by_sector):
    shape = (PARTS, PARTS)
    own = lax.broadcasted_iota(jnp.int32, shape, 1 if by_sector else 0)
    sector = lax.broadcasted_iota(jnp.int32, shape, 0 if by_sector else 1)
    ids = jnp.zeros(shape, jnp.int32)
    for d in range(PARTS):
        ids = jnp.where(own == d, perm_ref[d], ids)
    half, quarter = PARTS // 2, PARTS // 4
    even = ids <= half
    turn = jnp.where(even, ids, ids - half) * sector
    turn = (turn + jnp.where(even, 0, PARTS - quarter)) & (PARTS - 1)
    value = jnp.zeros(shape, F32)
    for n in range(PARTS):
        value = jnp.where(turn == n, math.cos(2.0 * math.pi * n / PARTS) if n % half != quarter else 0.0, value)
    ends = (ids == 0) | (ids == half)
    return value * jnp.where(ends, math.sqrt(1.0 / PARTS), math.sqrt(2.0 / PARTS))


def lanes_of(shape):
    return lax.broadcasted_iota(jnp.int32, shape, len(shape) - 1)


def source_row(rhs_ref, flux_ref, cell, start, count):
    row = rhs_ref[pl.ds(start * CELLS + cell, count, stride=CELLS), :]
    if cell // ROWS == DEPTH - 1:
        row = row + flux_ref[pl.ds(start * ROWS + cell % ROWS, count, stride=ROWS), :]
    return row


def sigma_of(table_ref, mat):
    sigma = jnp.zeros(mat.shape, F32)
    for m in range(8):
        sigma = jnp.where(mat == float(m), table_ref[m : m + 1, :], sigma)
    return sigma


def by_core(first, second):
    core = lax.axis_index("c")
    pl.when(core == 0)(first)
    pl.when(core == 1)(second)


def share_kernel(rhs_hbm, flux_hbm, mat_hbm, o_ref, rhs_ref, flux_ref, mat_ref, sem):
    copies = [
        pltpu.make_async_copy(rhs_hbm.at[:, pl.ds(CELLS - TALL, TALL), :], rhs_ref, sem.at[0]),
        pltpu.make_async_copy(flux_hbm, flux_ref, sem.at[1]),
        pltpu.make_async_copy(mat_hbm, mat_ref, sem.at[2]),
    ]
    for copy in copies:
        copy.start()
    for copy in copies:
        copy.wait()
    mat = mat_ref[CELLS - TALL : CELLS, :].astype(F32).astype(BF16)
    for e in range(EXC):
        k, own = e // MINE, e % MINE
        f = jnp.concatenate([jnp.zeros((TALL - ROWS, PTS), F32), flux_ref[e * ROWS : (e + 1) * ROWS, :]], 0)
        o_ref[k * PIECE + own * TALL : k * PIECE + (own + 1) * TALL, :] = (rhs_ref[e] + f).astype(BF16)
        if own == 0:
            o_ref[k * PIECE + MINE * TALL : (k + 1) * PIECE, :] = mat


def rim_kernel(x_ref, o_ref, near_ref, far_ref, f_ref):
    f_ref[...] = x_ref[...].astype(F32)
    for r in range(PIECE):
        o_ref[r * PARTS : (r + 1) * PARTS, :] = f_ref[pl.ds(r, PARTS, stride=PIECE), :].astype(BF16)

    def fill(top_ref, bot_ref):
        at = 0
        for d, k in RIM:
            for own in range(MINE + 1):
                top, bot = own * TALL + d * ROWS + k, own * TALL + d * ROWS + ROWS - 1 - k
                top_ref[at : at + PARTS, :] = o_ref[top * PARTS : (top + 1) * PARTS, :]
                bot_ref[at : at + PARTS, :] = o_ref[bot * PARTS : (bot + 1) * PARTS, :]
                at += PARTS

    by_core(lambda: fill(far_ref, near_ref), lambda: fill(near_ref, far_ref))


def take_sides(near_ref, far_ref, next_ref, prev_ref):
    def take(a, b):
        next_ref[...] = a[...]
        prev_ref[...] = b[...]

    by_core(lambda: take(near_ref, far_ref), lambda: take(far_ref, near_ref))


def trace_kernel(table_ref, x_ref, near_ref, far_ref, o_ref, f_ref, next_ref, prev_ref):
    take_sides(near_ref, far_ref, next_ref, prev_ref)

    def tile(own, d, z):
        if 0 <= z < ROWS:
            ref, at = x_ref, own * TALL + d * ROWS + z
        else:
            ref, k = (prev_ref, -1 - z) if z < 0 else (next_ref, z - ROWS)
            at = RIM.index((d, k)) * (MINE + 1) + own
        return ref[at * PARTS : (at + 1) * PARTS, :].astype(F32)

    top = SWEEPS - 1
    diagonal, inverse = {}, {}
    for d in range(SWEEPS):
        for z in range(-d, ROWS + d):
            diagonal[d, z] = 6.0 + sigma_of(table_ref, tile(MINE, d, z))
            inverse[d, z] = 1.0 / diagonal[d, z]
    lane = lanes_of((PARTS, PTS))

    def sides(v):
        a, b = pltpu.roll(v, 1, 1), pltpu.roll(v, PTS - 1, 1)
        a = jnp.where(lane == 0, pltpu.roll(a, 1, 0), a)
        b = jnp.where(lane == PTS - 1, pltpu.roll(b, PARTS - 1, 0), b)
        return a + b

    sigma_one = center / radius
    traces = []
    for own in range(MINE):
        r = {at: tile(own, *at) for at in diagonal}
        p = {at: r[at] * inverse[at] / center for at in diagonal}
        total = {z: p[top, z] for z in range(ROWS)}
        ratio_now = 1.0 / sigma_one
        for sweep in range(DEEP):
            ratio_next = 1.0 / (2.0 * sigma_one - ratio_now)
            keep, step = ratio_next * ratio_now, 2.0 * ratio_next / radius
            new = {}
            for d in range(sweep + 1, SWEEPS):
                reach = d - sweep - 1
                for z in range(-reach, ROWS + reach):
                    near = p[d - 1, z] + (p[d, z - 1] + p[d, z + 1]) + sides(p[d, z])
                    if d < top:
                        near = near + p[d + 1, z]
                    r[d, z] = r[d, z] - (diagonal[d, z] * p[d, z] - near)
                    new[d, z] = keep * p[d, z] + step * (r[d, z] * inverse[d, z])
            p, ratio_now = new, ratio_next
            total = {z: total[z] + p[top, z] for z in range(ROWS)}
        traces += [total[z].astype(BF16).astype(F32) for z in range(ROWS)]
    y = jnp.dot(table_ref[8:24, :PARTS], jnp.concatenate(traces, 1),
                precision=lax.Precision.HIGHEST, preferred_element_type=F32)
    for k in range(MINE * ROWS):
        f_ref[pl.ds(k, PARTS, stride=MINE * ROWS), :] = y[:, k * PTS : (k + 1) * PTS]
    out = f_ref[...].astype(BF16)
    o_ref[0:256, :] = out
    o_ref[256:512, :] = out


def roll(x, lanes):
    lanes %= PTS
    return pltpu.roll(x, lanes, 1) if lanes else x


def pack_edges(row, cell, low, high):
    lane = lanes_of(row.shape)
    for j in range(DEEP):
        low = jnp.where(lane == 4 * cell + 3 - j, roll(row, 4 * cell + 3 - 2 * j), low)
        high = jnp.where(lane == 4 * cell + j, roll(row, 4 * cell + 2 * j + 1), high)
    return low, high


def edge_kernel(coef_hbm, perm_hbm, rhs_hbm, flux_hbm, mat_hbm, low_ref, high_ref, near_ref, far_ref, table_ref,
                coef_ref, perm_ref, rhs_ref, flux_ref, mat_ref, sem):
    pairs = ((rhs_hbm, rhs_ref), (flux_hbm, flux_ref), (mat_hbm, mat_ref), (coef_hbm, coef_ref), (perm_hbm, perm_ref))
    copies = [pltpu.make_async_copy(*pair, sem.at[k]) for k, pair in enumerate(pairs)]
    for copy in copies:
        copy.start()
    for copy in copies:
        copy.wait()
    by_core(lambda: fill_slabs(rhs_ref, flux_ref, mat_ref, far_ref, near_ref),
            lambda: fill_slabs(rhs_ref, flux_ref, mat_ref, near_ref, far_ref))
    for m in range(8):
        table_ref[m : m + 1, :] = jnp.full((1, PTS), coef_ref[m], F32)
    for at, by_sector in ((8, False), (24, True)):
        table_ref[at : at + PARTS, :PARTS] = basis_of(perm_ref, by_sector)
    sides = (jnp.zeros((EXC, PTS), F32),) * 2
    mats = (jnp.zeros((1, PTS), F32),) * 2
    for cell in range(CELLS):
        sides = pack_edges(source_row(rhs_ref, flux_ref, cell, 0, EXC), cell, *sides)
        mats = pack_edges(mat_ref[cell : cell + 1, :].astype(F32), cell, *mats)
    for ref, side, mat in zip((low_ref, high_ref), sides, mats):
        ref[0:EXC, :] = side.astype(BF16)
        ref[EXC:EDGE, :] = jnp.broadcast_to(mat, (16, PTS)).astype(BF16)


def fill_slabs(rhs_ref, flux_ref, mat_ref, top_ref, bot_ref):
    mtop, mbot = [], []
    for d in range(DEPTH):
        for z in range(ROWS):
            cell = d * ROWS + z
            row = source_row(rhs_ref, flux_ref, cell, 0, EXC).astype(BF16)
            if z < DEEP:
                top_ref[pl.ds((d * DEEP + z) * EXC, EXC), :] = row
            if z >= ROWS - DEEP:
                bot_ref[pl.ds((d * DEEP + z - ROWS + DEEP) * EXC, EXC), :] = row
        mtop.append(mat_ref[d * ROWS : d * ROWS + DEEP, :].astype(F32))
        mbot.append(mat_ref[d * ROWS + ROWS - DEEP : (d + 1) * ROWS, :].astype(F32))
    pad = [jnp.zeros((32 - DEPTH * DEEP, PTS), F32)]
    top_ref[BULK : BULK + 32, :] = jnp.concatenate(mtop + pad, 0).astype(BF16)
    bot_ref[BULK : BULK + 32, :] = jnp.concatenate(mbot + pad, 0).astype(BF16)


def place_edges(halo, right, left, cell, z):
    lane = lanes_of(halo.shape)
    both = jnp.where(lane % 8 < 4, roll(right, 8 * z - 4 * cell), roll(left, 8 * z + 4 - 4 * cell))
    return jnp.where(lane // 8 == z, both, halo)


def sweep_kernel(part, count, table_ref, rhs_hbm, flux_hbm, mat_hbm, right_ref, left_ref, near_ref, far_ref, *refs):
    (out_hbm, dg_ref, iv_ref, r_ref, p0_ref, p1_ref, p2_ref, dgh_ref, ivh_ref, rh_ref, h0_ref, h1_ref, h2_ref,
     next_ref, prev_ref, sol_ref, rhs_ref, flux_ref, mat_ref, sem) = refs[count:]
    rows, at = GROUP * CELLS, part * GROUP
    copies = (pltpu.make_async_copy(mat_hbm, mat_ref, sem.at[0]),
              pltpu.make_async_copy(rhs_hbm.at[pl.ds(part * rows, rows), :], rhs_ref, sem.at[1]),
              pltpu.make_async_copy(flux_hbm.at[pl.ds(at * ROWS, GROUP * ROWS), :], flux_ref, sem.at[2]))
    for copy in copies:
        copy.start()
    take_sides(near_ref, far_ref, next_ref, prev_ref)
    copies[0].wait()

    def where_is(z):
        if z < DEEP:
            return prev_ref, z, z + ROWS - DEEP
        if z >= DEEP + ROWS:
            return next_ref, z - DEEP - ROWS, z - DEEP - ROWS
        return None, None, z - DEEP

    def edges(slab, at, count):
        if slab is None:
            return [ref[pl.ds(at, count), :].astype(F32) for ref in (right_ref, left_ref)]
        return [slab[pl.ds(BULK + 32 + off + at, count), :].astype(F32) for off in (0, EDGE)]

    for d in range(DEPTH):
        halo = jnp.zeros((16, PTS), F32)
        for z in range(WIDE):
            slab, k, own = where_is(z)
            cell = d * ROWS + own
            if slab is None:
                mid = mat_ref[cell : cell + 1, :].astype(F32)
            else:
                base, off = BULK + (d * DEEP + k) // 16 * 16, (d * DEEP + k) % 16
                mid = slab[base : base + 16, :].astype(F32)[off : off + 1, :]
            diagonal = 6.0 + sigma_of(table_ref, mid)
            dg_ref[d, z] = jnp.broadcast_to(diagonal, (8, PTS))
            iv_ref[d, z] = jnp.broadcast_to(1.0 / diagonal, (8, PTS))
            halo = place_edges(halo, *edges(slab, EXC, 16), cell, z)
        diagonal = 6.0 + sigma_of(table_ref, halo[0:8])
        dgh_ref[d] = diagonal
        ivh_ref[d] = 1.0 / diagonal

    zero = jnp.zeros((GROUP, PTS), F32)
    fields, halos = (p0_ref, p1_ref, p2_ref), (h0_ref, h1_ref, h2_ref)
    for field, halo in zip(fields, halos):
        for d in (0, DEPTH + 1):
            halo[d] = zero
            for z in range(WIDE):
                field[d, z] = zero

    def both(v):
        return jnp.concatenate([v, v], 0)

    lane = lanes_of((GROUP, PTS))
    spot = lane % 8

    def one_group():
        copies[1].wait()
        copies[2].wait()
        packed = {id(slab): edges(slab, at, GROUP) for slab in (None, next_ref, prev_ref)}
        for d in range(DEPTH):
            halo = zero
            for z in range(WIDE):
                slab, k, own = where_is(z)
                cell = d * ROWS + own
                if slab is None:
                    mid = source_row(rhs_ref, flux_ref, cell, 0, GROUP)
                else:
                    mid = slab[pl.ds((d * DEEP + k) * EXC + at, GROUP), :].astype(F32)
                halo = place_edges(halo, *packed[id(slab)], cell, z)
                r_ref[d, z] = mid
                p0_ref[d + 1, z] = mid * both(iv_ref[d, z]) / center
            rh_ref[d] = halo
            h0_ref[d + 1] = halo * both(ivh_ref[d]) / center
        sigma_one = center / radius
        ratio_now = 1.0 / sigma_one
        for sweep in range(DEEP):
            ratio_next = 1.0 / (2.0 * sigma_one - ratio_now)
            keep, step = ratio_next * ratio_now, 2.0 * ratio_next / radius
            last = sweep + 1 == DEEP

            def layer(d, carry, p=fields[sweep], h=halos[sweep], last=last, sweep=sweep, keep=keep, step=step):
                side = h[d + 1]
                ends = zero
                for z in range(1 + sweep, WIDE - 1 - sweep):
                    c = p[d + 1, z]
                    beside = roll(side, -8 * z - 4)
                    total = p[d, z] + p[d + 2, z]
                    total = total + (p[d + 1, z + 1] + p[d + 1, z - 1])
                    total = total + (jnp.where(lane == 0, beside, roll(c, 1)) + jnp.where(lane == PTS - 1, beside, roll(c, -1)))
                    r = r_ref[d, z] - (both(dg_ref[d, z]) * c - total)
                    new = keep * c + step * (r * both(iv_ref[d, z]))
                    if last:
                        out = (p0_ref[d + 1, z] + p1_ref[d + 1, z]) + c + new
                        sol_ref[pl.ds(d * ROWS + z - DEEP, GROUP, stride=CELLS), :] = out
                    else:
                        r_ref[d, z] = r
                        fields[sweep + 1][d + 1, z] = new
                        ends = jnp.where((lane == 8 * z + 3) | (lane == 8 * z + 4), roll(c, 8 * z + 4), ends)
                if not last:
                    total = h[d] + h[d + 2] + (roll(side, 8) + roll(side, -8)) + ends
                    total = total + (jnp.where(spot == 4, 0.0, roll(side, 1)) + jnp.where(spot == 3, 0.0, roll(side, -1)))
                    r = rh_ref[d] - (both(dgh_ref[d]) * side - total)
                    rh_ref[d] = r
                    halos[sweep + 1][d + 1] = keep * side + step * (r * both(ivh_ref[d]))
                return carry

            lax.fori_loop(0, DEPTH, layer, 0, unroll=4)
            ratio_now = ratio_next

    one_group()
    copy = pltpu.make_async_copy(sol_ref, out_hbm.at[pl.ds(part * rows, rows), :], sem.at[3])
    copy.start()
    copy.wait()


def flux_kernel(table_ref, x_ref, o_ref, f_ref):
    f_ref[...] = x_ref[...].astype(F32)
    x = jnp.concatenate([f_ref[pl.ds(r, PARTS, stride=PARTS), :] for r in range(PARTS)], 1)
    y = jnp.dot(table_ref[24:40, :PARTS], x, precision=lax.Precision.HIGHEST, preferred_element_type=F32)
    for r in range(PARTS):
        f_ref[pl.ds(r, PARTS, stride=PARTS), :] = y[:, r * PTS : (r + 1) * PTS]
    o_ref[...] = f_ref[...].astype(BF16)


def block_kernel(idx_ref, *refs):
    pieces, (w_ref, o_ref, wb_ref, f_ref, sem) = refs[:8], refs[8:]
    deep = ROWS * PTS

    def fetch(k):
        return pltpu.make_async_copy(
            w_ref.at[0, pl.ds(pl.multiple_of(idx_ref[k] * deep, deep), deep), :],
            wb_ref.at[pl.ds(k * deep, deep), :], sem.at[k])

    for k in range(16):
        fetch(k).start()
    for k in range(16):
        f_ref[pl.ds(k * 256, 256), :] = pieces[k // 2][k % 2].astype(F32)
    acc = jnp.zeros((EXC, 512), F32)
    for k in range(16):
        x = jnp.concatenate([f_ref[pl.ds(k * 256 + z, EXC, stride=ROWS), :] for z in range(ROWS)], 1)
        fetch(k).wait()
        acc = acc + jnp.dot(x.astype(BF16), wb_ref[pl.ds(k * deep, deep), :], preferred_element_type=F32)
    for z in range(ROWS):
        f_ref[pl.ds(z, EXC, stride=ROWS), :] = acc[:, z * PTS : (z + 1) * PTS]
    o_ref[...] = f_ref[0:256, :].astype(BF16)


def shape(rows, dtype=BF16, cols=PTS):
    return jax.ShapeDtypeStruct((rows, cols), dtype)


def call(kernel, out, ins, scratch=(), mib=8, **more):
    outs = out if isinstance(out, tuple) else (out,)
    kernel_call = pl.pallas_call(
        kernel, out_shape=outs, in_specs=list(ins), scratch_shapes=list(scratch),
        **({"out_specs": (VMEM,) * len(outs)} | more),
        compiler_params=pltpu.CompilerParams(vmem_limit_bytes=mib << 20))

    def got(*args):
        return kernel_call(*args)

    return got if isinstance(out, tuple) else (lambda *args: got(*args)[0])


def in_hbm(x):
    return pltpu.with_memory_space_constraint(x, pltpu.HBM)


def exchange(x):
    return lax.all_to_all(x.reshape(PARTS, -1, PTS), SEC, 0, 0, tiled=True).reshape(-1, PTS)


def response_of(pair, blocks):
    y, c = lax.axis_index("y"), lax.axis_index("c")

    def rows(k, core):
        return [a * 8 + (y - k) % 4 * 2 + core for a in (0, 1)]

    def swap(v):
        return lax.ppermute(v, "c", [(0, 1), (1, 0)])

    moved = {k: lax.ppermute(pair, "y", [(i, (i + k) % 4) for i in range(4)]) for k in (1, 3, 2)}
    moved[0] = pair
    pieces, index = [], []
    for k in (0, 1, 3, 2):
        pieces += [moved[k], swap(moved[k])]
        index += rows(k, c) + rows(k, 1 - c)
    return call(
        block_kernel, shape(256), [SMEM] + [VMEM] * 8 + [HBM],
        [pltpu.VMEM((8192, 512), BF16), pltpu.VMEM((16 * 256, PTS), F32), pltpu.SemaphoreType.DMA((16,))], mib=16,
    )(jnp.stack(index).astype(jnp.int32), *pieces, in_hbm(blocks))


def per_device(rhs, flux_in, materials, mat_coef, owner_perm, blocks):
    rhs2 = rhs.reshape(EXC * CELLS, PTS)
    flux2 = flux_in.reshape(EXC * ROWS, PTS)
    mat2 = materials.reshape(CELLS, PTS)
    ring = [(i, (i + 1) % 16) for i in range(16)]
    back = [((i + 1) % 16, i) for i in range(16)]
    tie = lax.optimization_barrier

    def near(x):
        return lax.ppermute(x, VOL, [(i, i ^ 1) for i in range(16)])

    def far(x):
        return lax.ppermute(x, VOL, [(i, (i + 1 if i % 2 else i - 1) % 16) for i in range(16)])

    shared = exchange(call(
        share_kernel, shape(PARTS * PIECE), [HBM] * 3,
        [pltpu.VMEM((EXC, TALL, PTS), F32), pltpu.VMEM((EXC * ROWS, PTS), F32), pltpu.VMEM((CELLS, PTS), jnp.int32),
         pltpu.SemaphoreType.DMA((3,))],
    )(*map(in_hbm, (rhs.reshape(EXC, CELLS, PTS), flux2, mat2))))
    low, high, near_slab, far_slab, table = call(
        edge_kernel, (shape(EDGE), shape(EDGE), shape(SLAB), shape(SLAB), shape(40, F32)), [HBM] * 5,
        [pltpu.SMEM((8,), F32), pltpu.SMEM((PARTS,), jnp.int32), pltpu.VMEM((EXC * CELLS, PTS), F32),
         pltpu.VMEM((EXC * ROWS, PTS), F32), pltpu.VMEM((CELLS, PTS), jnp.int32), pltpu.SemaphoreType.DMA((5,))],
    )(*map(in_hbm, (mat_coef, owner_perm, rhs2, flux2, mat2)))
    right = lax.ppermute(low, SEC, back)
    left = lax.ppermute(high, SEC, ring)
    shared, near_slab, far_slab, table = tie((shared, near_slab, far_slab, table))

    rim = shape(len(RIM) * (MINE + 1) * PARTS)
    own, near_rim, far_rim = call(
        rim_kernel, (shape(PARTS * PIECE), rim, rim), [VMEM], [pltpu.VMEM((PARTS * PIECE, PTS), F32)])(shared)
    far_rim, near_rim = far(far_rim), near(near_rim)
    sides = jnp.concatenate([right, left])
    near_slab = lax.dynamic_update_slice(near_slab, sides, (BULK + 32, 0))
    far_slab = lax.dynamic_update_slice(far_slab, sides, (BULK + 32, 0))
    near_slab, far_slab = near(near_slab), far(far_slab)
    harmonics = call(
        trace_kernel, shape(512), [VMEM] * 4, [pltpu.VMEM((256, PTS), F32)] + [pltpu.VMEM(rim.shape, BF16)] * 2,
    )(table, own, near_rim, far_rim)
    pair = lax.all_to_all(harmonics.reshape(32, 16, PTS), ("zh",) + SEC, 0, 0, tiled=True).reshape(2, 256, PTS)
    response = response_of(pair, blocks)
    response = exchange(response)

    wide, tall = (DEPTH, WIDE, GROUP, PTS), (DEPTH + 2, WIDE, GROUP, PTS)
    scratch = [(DEPTH, WIDE, 8, PTS)] * 2 + [wide] + [tall] * 3
    scratch += [(DEPTH, 8, PTS)] * 2 + [(DEPTH, GROUP, PTS)] + [(DEPTH + 2, GROUP, PTS)] * 3
    scratch = [pltpu.VMEM(size, F32) for size in scratch] + [pltpu.VMEM((SLAB, PTS), BF16)] * 2
    scratch += [pltpu.VMEM((GROUP * CELLS, PTS), F32)] * 2
    scratch += [pltpu.VMEM((GROUP * ROWS, PTS), F32), pltpu.VMEM((CELLS, PTS), jnp.int32), pltpu.SemaphoreType.DMA((4,))]

    args = (table, *map(in_hbm, (rhs2, flux2, mat2)), right, left, near_slab, far_slab)
    solution = None
    for part in range(EXC // GROUP):
        more = [] if solution is None else [solution]
        specs = [VMEM] + [HBM] * 3 + [VMEM] * 4 + [HBM] * len(more)
        solution = call(
            lambda *refs, part=part, count=len(more): sweep_kernel(part, count, *refs), shape(EXC * CELLS, F32), specs, scratch,
            mib=16, out_specs=(HBM,), input_output_aliases={8: 0} if part else {},
        )(*args, *more)
    flux = call(flux_kernel, shape(256), [VMEM] * 2, [pltpu.VMEM((256, PTS), F32)])(table, response)
    flux = exchange(flux)
    return solution.reshape(EXC, DEPTH, ROWS, PTS), flux.astype(F32).reshape(EXC, ROWS, PTS)


def solution(mesh):
    fine = jax.sharding.Mesh(mesh.devices.reshape(2, 4, 2, 4, 4), VOL + SEC)
    return jax.shard_map(
        per_device,
        mesh=fine,
        in_specs=(P(None, None, VOL, SEC), P(None, VOL, SEC), P(None, VOL, SEC), P(), P(), P(SEC, None, VOL)),
        out_specs=(P(None, None, VOL, SEC), P(None, VOL, SEC)),
        check_vma=False,
    )
```

```python
import math

import jax
import jax.numpy as jnp
from jax import lax
from jax.experimental import pallas as pl
from jax.experimental.pallas import tpu as pltpu
from jax.sharding import PartitionSpec as P

SWEEPS = 4
DEEP = SWEEPS - 1

center = 1.0
radius = 0.93

F32 = jnp.float32
BF16 = jnp.bfloat16
SMEM = pl.BlockSpec(memory_space=pltpu.SMEM)
VMEM = pl.BlockSpec(memory_space=pltpu.VMEM)
HBM = pl.BlockSpec(memory_space=pltpu.HBM)

EXC, DEPTH, ROWS, PTS, PARTS = 64, 8, 4, 128, 16
CELLS = DEPTH * ROWS
EDGE = EXC + 16
BULK = DEPTH * DEEP * EXC
SLAB = BULK + 32 + 2 * EDGE
GROUP = 16
WIDE = ROWS + 2 * DEEP
TALL = SWEEPS * ROWS
MINE = EXC // PARTS
PIECE = TALL * (MINE + 1)
RIM = [(d, k) for d in range(SWEEPS - 1, 0, -1) for k in range(d)]

VOL = ("zh", "y", "c")
SEC = ("zl", "x")


def basis_of(perm_ref):
    shape = (PARTS, PARTS)
    own = lax.broadcasted_iota(jnp.int32, shape, 0)
    sector = lax.broadcasted_iota(jnp.int32, shape, 1)
    ids = jnp.zeros(shape, jnp.int32)
    for d in range(PARTS):
        ids = jnp.where(own == d, perm_ref[d], ids)
    half, quarter = PARTS // 2, PARTS // 4
    even = ids <= half
    turn = jnp.where(even, ids, ids - half) * sector
    turn = (turn + jnp.where(even, 0, PARTS - quarter)) & (PARTS - 1)
    value = jnp.zeros(shape, F32)
    for n in range(PARTS):
        value = jnp.where(turn == n, math.cos(2.0 * math.pi * n / PARTS) if n % half != quarter else 0.0, value)
    ends = (ids == 0) | (ids == half)
    return value * jnp.where(ends, math.sqrt(1.0 / PARTS), math.sqrt(2.0 / PARTS))


def lanes_of(shape):
    return lax.broadcasted_iota(jnp.int32, shape, len(shape) - 1)


def source_row(rhs_ref, flux_ref, cell, start, count):
    row = rhs_ref[pl.ds(start * CELLS + cell, count, stride=CELLS), :]
    if cell // ROWS == DEPTH - 1:
        row = row + flux_ref[pl.ds(start * ROWS + cell % ROWS, count, stride=ROWS), :]
    return row


def sigma_of(table_ref, mat):
    sigma = jnp.zeros(mat.shape, F32)
    for m in range(8):
        sigma = jnp.where(mat == float(m), table_ref[m : m + 1, :], sigma)
    return sigma


def by_core(first, second):
    core = lax.axis_index("c")
    pl.when(core == 0)(first)
    pl.when(core == 1)(second)


def share_kernel(rhs_hbm, flux_hbm, mat_hbm, o_ref, rhs_ref, flux_ref, mat_ref, sem):
    copies = [
        pltpu.make_async_copy(rhs_hbm.at[:, pl.ds(CELLS - TALL, TALL), :], rhs_ref, sem.at[0]),
        pltpu.make_async_copy(flux_hbm, flux_ref, sem.at[1]),
        pltpu.make_async_copy(mat_hbm, mat_ref, sem.at[2]),
    ]
    for copy in copies:
        copy.start()
    for copy in copies:
        copy.wait()
    mat = mat_ref[CELLS - TALL : CELLS, :].astype(F32).astype(BF16)
    for e in range(EXC):
        k, own = e // MINE, e % MINE
        f = jnp.concatenate([jnp.zeros((TALL - ROWS, PTS), F32), flux_ref[e * ROWS : (e + 1) * ROWS, :]], 0)
        o_ref[k * PIECE + own * TALL : k * PIECE + (own + 1) * TALL, :] = (rhs_ref[e] + f).astype(BF16)
        if own == 0:
            o_ref[k * PIECE + MINE * TALL : (k + 1) * PIECE, :] = mat


def rim_kernel(x_ref, o_ref, near_ref, far_ref, f_ref):
    f_ref[...] = x_ref[...].astype(F32)
    for r in range(PIECE):
        o_ref[r * PARTS : (r + 1) * PARTS, :] = f_ref[pl.ds(r, PARTS, stride=PIECE), :].astype(BF16)

    def fill(top_ref, bot_ref):
        at = 0
        for d, k in RIM:
            for own in range(MINE + 1):
                top, bot = own * TALL + d * ROWS + k, own * TALL + d * ROWS + ROWS - 1 - k
                top_ref[at : at + PARTS, :] = o_ref[top * PARTS : (top + 1) * PARTS, :]
                bot_ref[at : at + PARTS, :] = o_ref[bot * PARTS : (bot + 1) * PARTS, :]
                at += PARTS

    by_core(lambda: fill(far_ref, near_ref), lambda: fill(near_ref, far_ref))


def take_sides(near_ref, far_ref, next_ref, prev_ref):
    def take(a, b):
        next_ref[...] = a[...]
        prev_ref[...] = b[...]

    by_core(lambda: take(near_ref, far_ref), lambda: take(far_ref, near_ref))


def trace_kernel(table_ref, x_ref, near_ref, far_ref, o_ref, f_ref, next_ref, prev_ref):
    take_sides(near_ref, far_ref, next_ref, prev_ref)

    def tile(own, d, z):
        if 0 <= z < ROWS:
            ref, at = x_ref, own * TALL + d * ROWS + z
        else:
            ref, k = (prev_ref, -1 - z) if z < 0 else (next_ref, z - ROWS)
            at = RIM.index((d, k)) * (MINE + 1) + own
        return ref[at * PARTS : (at + 1) * PARTS, :].astype(F32)

    top = SWEEPS - 1
    diagonal, inverse = {}, {}
    for d in range(SWEEPS):
        for z in range(-d, ROWS + d):
            diagonal[d, z] = 6.0 + sigma_of(table_ref, tile(MINE, d, z))
            inverse[d, z] = 1.0 / diagonal[d, z]
    lane = lanes_of((PARTS, PTS))

    def sides(v):
        a, b = pltpu.roll(v, 1, 1), pltpu.roll(v, PTS - 1, 1)
        a = jnp.where(lane == 0, pltpu.roll(a, 1, 0), a)
        b = jnp.where(lane == PTS - 1, pltpu.roll(b, PARTS - 1, 0), b)
        return a + b

    sigma_one = center / radius
    traces = []
    for own in range(MINE):
        r = {at: tile(own, *at) for at in diagonal}
        p = {at: r[at] * inverse[at] / center for at in diagonal}
        total = {z: p[top, z] for z in range(ROWS)}
        ratio_now = 1.0 / sigma_one
        for sweep in range(DEEP):
            ratio_next = 1.0 / (2.0 * sigma_one - ratio_now)
            keep, step = ratio_next * ratio_now, 2.0 * ratio_next / radius
            new = {}
            for d in range(sweep + 1, SWEEPS):
                reach = d - sweep - 1
                for z in range(-reach, ROWS + reach):
                    near = p[d - 1, z] + (p[d, z - 1] + p[d, z + 1]) + sides(p[d, z])
                    if d < top:
                        near = near + p[d + 1, z]
                    r[d, z] = r[d, z] - (diagonal[d, z] * p[d, z] - near)
                    new[d, z] = keep * p[d, z] + step * (r[d, z] * inverse[d, z])
            p, ratio_now = new, ratio_next
            total = {z: total[z] + p[top, z] for z in range(ROWS)}
        traces += [total[z].astype(BF16).astype(F32) for z in range(ROWS)]
    y = jnp.dot(table_ref[8:24, :PARTS], jnp.concatenate(traces, 1),
                precision=lax.Precision.HIGHEST, preferred_element_type=F32)
    for k in range(MINE * ROWS):
        f_ref[pl.ds(k, PARTS, stride=MINE * ROWS), :] = y[:, k * PTS : (k + 1) * PTS]
    out = f_ref[...].astype(BF16)
    o_ref[0:256, :] = out
    o_ref[256:512, :] = out


def roll(x, lanes):
    lanes %= PTS
    return pltpu.roll(x, lanes, 1) if lanes else x


def pack_edges(row, cell, low, high):
    lane = lanes_of(row.shape)
    for j in range(DEEP):
        low = jnp.where(lane == 4 * cell + 3 - j, roll(row, 4 * cell + 3 - 2 * j), low)
        high = jnp.where(lane == 4 * cell + j, roll(row, 4 * cell + 2 * j + 1), high)
    return low, high


def edge_kernel(coef_hbm, perm_hbm, rhs_hbm, flux_hbm, mat_hbm, low_ref, high_ref, near_ref, far_ref, table_ref,
                coef_ref, perm_ref, rhs_ref, flux_ref, mat_ref, sem):
    pairs = ((rhs_hbm, rhs_ref), (flux_hbm, flux_ref), (mat_hbm, mat_ref), (coef_hbm, coef_ref), (perm_hbm, perm_ref))
    copies = [pltpu.make_async_copy(*pair, sem.at[k]) for k, pair in enumerate(pairs)]
    for copy in copies:
        copy.start()
    for copy in copies:
        copy.wait()
    by_core(lambda: fill_slabs(rhs_ref, flux_ref, mat_ref, far_ref, near_ref),
            lambda: fill_slabs(rhs_ref, flux_ref, mat_ref, near_ref, far_ref))
    for m in range(8):
        table_ref[m : m + 1, :] = jnp.full((1, PTS), coef_ref[m], F32)
    table_ref[8:24, :PARTS] = basis_of(perm_ref)
    row, col = lax.axis_index("zl"), lax.axis_index("x")
    lane = lanes_of((1, PTS))
    for k in range(4):
        of_owner = table_ref[pl.ds(8 + row * 4 + (col + 4 - k) % 4, 1), :]
        for j in range(4):
            weight = jnp.sum(jnp.where(lane == (row + j) % 4 * 4 + col, of_owner, 0.0), axis=1, keepdims=True)
            table_ref[24 + 4 * k + j : 25 + 4 * k + j, :] = jnp.broadcast_to(weight, (1, PTS))
    sides = (jnp.zeros((EXC, PTS), F32),) * 2
    mats = (jnp.zeros((1, PTS), F32),) * 2
    for cell in range(CELLS):
        sides = pack_edges(source_row(rhs_ref, flux_ref, cell, 0, EXC), cell, *sides)
        mats = pack_edges(mat_ref[cell : cell + 1, :].astype(F32), cell, *mats)
    for ref, side, mat in zip((low_ref, high_ref), sides, mats):
        ref[0:EXC, :] = side.astype(BF16)
        ref[EXC:EDGE, :] = jnp.broadcast_to(mat, (16, PTS)).astype(BF16)


def fill_slabs(rhs_ref, flux_ref, mat_ref, top_ref, bot_ref):
    mtop, mbot = [], []
    for d in range(DEPTH):
        for z in range(ROWS):
            cell = d * ROWS + z
            row = source_row(rhs_ref, flux_ref, cell, 0, EXC).astype(BF16)
            if z < DEEP:
                top_ref[pl.ds((d * DEEP + z) * EXC, EXC), :] = row
            if z >= ROWS - DEEP:
                bot_ref[pl.ds((d * DEEP + z - ROWS + DEEP) * EXC, EXC), :] = row
        mtop.append(mat_ref[d * ROWS : d * ROWS + DEEP, :].astype(F32))
        mbot.append(mat_ref[d * ROWS + ROWS - DEEP : (d + 1) * ROWS, :].astype(F32))
    pad = [jnp.zeros((32 - DEPTH * DEEP, PTS), F32)]
    top_ref[BULK : BULK + 32, :] = jnp.concatenate(mtop + pad, 0).astype(BF16)
    bot_ref[BULK : BULK + 32, :] = jnp.concatenate(mbot + pad, 0).astype(BF16)


def place_edges(halo, right, left, cell, z):
    lane = lanes_of(halo.shape)
    both = jnp.where(lane % 8 < 4, roll(right, 8 * z - 4 * cell), roll(left, 8 * z + 4 - 4 * cell))
    return jnp.where(lane // 8 == z, both, halo)


def sweep_kernel(part, count, table_ref, rhs_hbm, flux_hbm, mat_hbm, right_ref, left_ref, near_ref, far_ref, *refs):
    (out_hbm, dg_ref, iv_ref, r_ref, p0_ref, p1_ref, p2_ref, dgh_ref, ivh_ref, rh_ref, h0_ref, h1_ref, h2_ref,
     next_ref, prev_ref, sol_ref, rhs_ref, flux_ref, mat_ref, sem) = refs[count:]
    rows, at = GROUP * CELLS, part * GROUP
    copies = (pltpu.make_async_copy(mat_hbm, mat_ref, sem.at[0]),
              pltpu.make_async_copy(rhs_hbm.at[pl.ds(part * rows, rows), :], rhs_ref, sem.at[1]),
              pltpu.make_async_copy(flux_hbm.at[pl.ds(at * ROWS, GROUP * ROWS), :], flux_ref, sem.at[2]))
    for copy in copies:
        copy.start()
    take_sides(near_ref, far_ref, next_ref, prev_ref)
    copies[0].wait()

    def where_is(z):
        if z < DEEP:
            return prev_ref, z, z + ROWS - DEEP
        if z >= DEEP + ROWS:
            return next_ref, z - DEEP - ROWS, z - DEEP - ROWS
        return None, None, z - DEEP

    def edges(slab, at, count):
        if slab is None:
            return [ref[pl.ds(at, count), :].astype(F32) for ref in (right_ref, left_ref)]
        return [slab[pl.ds(BULK + 32 + off + at, count), :].astype(F32) for off in (0, EDGE)]

    for d in range(DEPTH):
        halo = jnp.zeros((16, PTS), F32)
        for z in range(WIDE):
            slab, k, own = where_is(z)
            cell = d * ROWS + own
            if slab is None:
                mid = mat_ref[cell : cell + 1, :].astype(F32)
            else:
                base, off = BULK + (d * DEEP + k) // 16 * 16, (d * DEEP + k) % 16
                mid = slab[base : base + 16, :].astype(F32)[off : off + 1, :]
            diagonal = 6.0 + sigma_of(table_ref, mid)
            dg_ref[d, z] = jnp.broadcast_to(diagonal, (8, PTS))
            iv_ref[d, z] = jnp.broadcast_to(1.0 / diagonal, (8, PTS))
            halo = place_edges(halo, *edges(slab, EXC, 16), cell, z)
        diagonal = 6.0 + sigma_of(table_ref, halo[0:8])
        dgh_ref[d] = diagonal
        ivh_ref[d] = 1.0 / diagonal

    zero = jnp.zeros((GROUP, PTS), F32)
    fields, halos = (p0_ref, p1_ref, p2_ref), (h0_ref, h1_ref, h2_ref)
    for field, halo in zip(fields, halos):
        for d in (0, DEPTH + 1):
            halo[d] = zero
            for z in range(WIDE):
                field[d, z] = zero

    def both(v):
        return jnp.concatenate([v, v], 0)

    lane = lanes_of((GROUP, PTS))
    spot = lane % 8

    def one_group():
        copies[1].wait()
        copies[2].wait()
        packed = {id(slab): edges(slab, at, GROUP) for slab in (None, next_ref, prev_ref)}
        for d in range(DEPTH):
            halo = zero
            for z in range(WIDE):
                slab, k, own = where_is(z)
                cell = d * ROWS + own
                if slab is None:
                    mid = source_row(rhs_ref, flux_ref, cell, 0, GROUP)
                else:
                    mid = slab[pl.ds((d * DEEP + k) * EXC + at, GROUP), :].astype(F32)
                halo = place_edges(halo, *packed[id(slab)], cell, z)
                r_ref[d, z] = mid
                p0_ref[d + 1, z] = mid * both(iv_ref[d, z]) / center
            rh_ref[d] = halo
            h0_ref[d + 1] = halo * both(ivh_ref[d]) / center
        sigma_one = center / radius
        ratio_now = 1.0 / sigma_one
        for sweep in range(DEEP):
            ratio_next = 1.0 / (2.0 * sigma_one - ratio_now)
            keep, step = ratio_next * ratio_now, 2.0 * ratio_next / radius
            last = sweep + 1 == DEEP

            def layer(d, carry, p=fields[sweep], h=halos[sweep], last=last, sweep=sweep, keep=keep, step=step):
                side = h[d + 1]
                ends = zero
                for z in range(1 + sweep, WIDE - 1 - sweep):
                    c = p[d + 1, z]
                    beside = roll(side, -8 * z - 4)
                    total = p[d, z] + p[d + 2, z]
                    total = total + (p[d + 1, z + 1] + p[d + 1, z - 1])
                    total = total + (jnp.where(lane == 0, beside, roll(c, 1)) + jnp.where(lane == PTS - 1, beside, roll(c, -1)))
                    r = r_ref[d, z] - (both(dg_ref[d, z]) * c - total)
                    new = keep * c + step * (r * both(iv_ref[d, z]))
                    if last:
                        out = (p0_ref[d + 1, z] + p1_ref[d + 1, z]) + c + new
                        sol_ref[pl.ds(d * ROWS + z - DEEP, GROUP, stride=CELLS), :] = out
                    else:
                        r_ref[d, z] = r
                        fields[sweep + 1][d + 1, z] = new
                        ends = jnp.where((lane == 8 * z + 3) | (lane == 8 * z + 4), roll(c, 8 * z + 4), ends)
                if not last:
                    total = h[d] + h[d + 2] + (roll(side, 8) + roll(side, -8)) + ends
                    total = total + (jnp.where(spot == 4, 0.0, roll(side, 1)) + jnp.where(spot == 3, 0.0, roll(side, -1)))
                    r = rh_ref[d] - (both(dgh_ref[d]) * side - total)
                    rh_ref[d] = r
                    halos[sweep + 1][d + 1] = keep * side + step * (r * both(ivh_ref[d]))
                return carry

            lax.fori_loop(0, DEPTH, layer, 0, unroll=4)
            ratio_now = ratio_next

    one_group()
    copy = pltpu.make_async_copy(sol_ref, out_hbm.at[pl.ds(part * rows, rows), :], sem.at[3])
    copy.start()
    copy.wait()


def partial_kernel(table_ref, *refs):
    pieces, outs = refs[:4], refs[4:]
    for j in range(4):
        total = jnp.zeros((256, PTS), F32)
        for k in range(4):
            total = total + table_ref[24 + 4 * k + j : 25 + 4 * k + j, :] * pieces[k][...].astype(F32)
        outs[j][...] = total.astype(outs[j].dtype)


def total_kernel(own_ref, *refs):
    total = own_ref[...]
    for ref in refs[:3]:
        total = total + ref[...].astype(F32)
    refs[3][...] = total


def block_kernel(idx_ref, *refs):
    pieces, (w_ref, o_ref, wb_ref, f_ref, sem) = refs[:8], refs[8:]
    deep = ROWS * PTS

    def fetch(k):
        return pltpu.make_async_copy(
            w_ref.at[0, pl.ds(pl.multiple_of(idx_ref[k] * deep, deep), deep), :],
            wb_ref.at[pl.ds(k * deep, deep), :], sem.at[k])

    for k in range(16):
        fetch(k).start()
    for k in range(16):
        f_ref[pl.ds(k * 256, 256), :] = pieces[k // 2][k % 2].astype(F32)
    acc = jnp.zeros((EXC, 512), F32)
    for k in range(16):
        x = jnp.concatenate([f_ref[pl.ds(k * 256 + z, EXC, stride=ROWS), :] for z in range(ROWS)], 1)
        fetch(k).wait()
        acc = acc + jnp.dot(x.astype(BF16), wb_ref[pl.ds(k * deep, deep), :], preferred_element_type=F32)
    for z in range(ROWS):
        f_ref[pl.ds(z, EXC, stride=ROWS), :] = acc[:, z * PTS : (z + 1) * PTS]
    o_ref[...] = f_ref[0:256, :].astype(BF16)


def shape(rows, dtype=BF16, cols=PTS):
    return jax.ShapeDtypeStruct((rows, cols), dtype)


def call(kernel, out, ins, scratch=(), mib=8, **more):
    outs = out if isinstance(out, tuple) else (out,)
    kernel_call = pl.pallas_call(
        kernel, out_shape=outs, in_specs=list(ins), scratch_shapes=list(scratch),
        **({"out_specs": (VMEM,) * len(outs)} | more),
        compiler_params=pltpu.CompilerParams(vmem_limit_bytes=mib << 20))

    def got(*args):
        return kernel_call(*args)

    return got if isinstance(out, tuple) else (lambda *args: got(*args)[0])


def in_hbm(x):
    return pltpu.with_memory_space_constraint(x, pltpu.HBM)


def exchange(x):
    return lax.all_to_all(x.reshape(PARTS, -1, PTS), SEC, 0, 0, tiled=True).reshape(-1, PTS)


def response_of(pair, blocks):
    y, c = lax.axis_index("y"), lax.axis_index("c")

    def rows(k, core):
        return [a * 8 + (y - k) % 4 * 2 + core for a in (0, 1)]

    def swap(v):
        return lax.ppermute(v, "c", [(0, 1), (1, 0)])

    moved = {k: lax.ppermute(pair, "y", [(i, (i + k) % 4) for i in range(4)]) for k in (1, 3, 2)}
    moved[0] = pair
    pieces, index = [], []
    for k in (0, 1, 3, 2):
        pieces += [moved[k], swap(moved[k])]
        index += rows(k, c) + rows(k, 1 - c)
    return call(
        block_kernel, shape(256), [SMEM] + [VMEM] * 8 + [HBM],
        [pltpu.VMEM((8192, 512), BF16), pltpu.VMEM((16 * 256, PTS), F32), pltpu.SemaphoreType.DMA((16,))], mib=16,
    )(jnp.stack(index).astype(jnp.int32), *pieces, in_hbm(blocks))


def per_device(rhs, flux_in, materials, mat_coef, owner_perm, blocks):
    rhs2 = rhs.reshape(EXC * CELLS, PTS)
    flux2 = flux_in.reshape(EXC * ROWS, PTS)
    mat2 = materials.reshape(CELLS, PTS)
    ring = [(i, (i + 1) % 16) for i in range(16)]
    back = [((i + 1) % 16, i) for i in range(16)]
    tie = lax.optimization_barrier

    def near(x):
        return lax.ppermute(x, VOL, [(i, i ^ 1) for i in range(16)])

    def far(x):
        return lax.ppermute(x, VOL, [(i, (i + 1 if i % 2 else i - 1) % 16) for i in range(16)])

    shared = exchange(call(
        share_kernel, shape(PARTS * PIECE), [HBM] * 3,
        [pltpu.VMEM((EXC, TALL, PTS), F32), pltpu.VMEM((EXC * ROWS, PTS), F32), pltpu.VMEM((CELLS, PTS), jnp.int32),
         pltpu.SemaphoreType.DMA((3,))],
    )(*map(in_hbm, (rhs.reshape(EXC, CELLS, PTS), flux2, mat2))))
    low, high, near_slab, far_slab, table = call(
        edge_kernel, (shape(EDGE), shape(EDGE), shape(SLAB), shape(SLAB), shape(40, F32)), [HBM] * 5,
        [pltpu.SMEM((8,), F32), pltpu.SMEM((PARTS,), jnp.int32), pltpu.VMEM((EXC * CELLS, PTS), F32),
         pltpu.VMEM((EXC * ROWS, PTS), F32), pltpu.VMEM((CELLS, PTS), jnp.int32), pltpu.SemaphoreType.DMA((5,))],
    )(*map(in_hbm, (mat_coef, owner_perm, rhs2, flux2, mat2)))
    right = lax.ppermute(low, SEC, back)
    left = lax.ppermute(high, SEC, ring)
    shared, near_slab, far_slab, table = tie((shared, near_slab, far_slab, table))

    rim = shape(len(RIM) * (MINE + 1) * PARTS)
    own, near_rim, far_rim = call(
        rim_kernel, (shape(PARTS * PIECE), rim, rim), [VMEM], [pltpu.VMEM((PARTS * PIECE, PTS), F32)])(shared)
    far_rim, near_rim = far(far_rim), near(near_rim)
    sides = jnp.concatenate([right, left])
    near_slab = lax.dynamic_update_slice(near_slab, sides, (BULK + 32, 0))
    far_slab = lax.dynamic_update_slice(far_slab, sides, (BULK + 32, 0))
    near_slab, far_slab = near(near_slab), far(far_slab)
    harmonics = call(
        trace_kernel, shape(512), [VMEM] * 4, [pltpu.VMEM((256, PTS), F32)] + [pltpu.VMEM(rim.shape, BF16)] * 2,
    )(table, own, near_rim, far_rim)
    pair = lax.all_to_all(harmonics.reshape(32, 16, PTS), ("zh",) + SEC, 0, 0, tiled=True).reshape(2, 256, PTS)
    response = response_of(pair, blocks)

    def turn(x, axis, k):
        return lax.ppermute(x, axis, [(i, (i + k) % 4) for i in range(4)])

    owners = {k: turn(response, "x", k) for k in (1, 3, 2)}
    own_part, *parts = call(
        partial_kernel, (shape(256, F32),) + (shape(256),) * 3, [VMEM] * 5,
    )(table, response, owners[1], owners[2], owners[3])
    parts = [turn(part, "zl", j) for j, part in zip((1, 2, 3), parts)]
    flux = call(total_kernel, shape(256, F32), [VMEM] * 4)(own_part, *parts)

    wide, tall = (DEPTH, WIDE, GROUP, PTS), (DEPTH + 2, WIDE, GROUP, PTS)
    scratch = [(DEPTH, WIDE, 8, PTS)] * 2 + [wide] + [tall] * 3
    scratch += [(DEPTH, 8, PTS)] * 2 + [(DEPTH, GROUP, PTS)] + [(DEPTH + 2, GROUP, PTS)] * 3
    scratch = [pltpu.VMEM(size, F32) for size in scratch] + [pltpu.VMEM((SLAB, PTS), BF16)] * 2
    scratch += [pltpu.VMEM((GROUP * CELLS, PTS), F32)] * 2
    scratch += [pltpu.VMEM((GROUP * ROWS, PTS), F32), pltpu.VMEM((CELLS, PTS), jnp.int32), pltpu.SemaphoreType.DMA((4,))]

    args = (table, *map(in_hbm, (rhs2, flux2, mat2)), right, left, near_slab, far_slab)
    solution = None
    for part in range(EXC // GROUP):
        more = [] if solution is None else [solution]
        specs = [VMEM] + [HBM] * 3 + [VMEM] * 4 + [HBM] * len(more)
        solution = call(
            lambda *refs, part=part, count=len(more): sweep_kernel(part, count, *refs), shape(EXC * CELLS, F32), specs, scratch,
            mib=16, out_specs=(HBM,), input_output_aliases={8: 0} if part else {},
        )(*args, *more)
    return solution.reshape(EXC, DEPTH, ROWS, PTS), flux.reshape(EXC, ROWS, PTS)


def solution(mesh):
    fine = jax.sharding.Mesh(mesh.devices.reshape(2, 4, 2, 4, 4), VOL + SEC)
    return jax.shard_map(
        per_device,
        mesh=fine,
        in_specs=(P(None, None, VOL, SEC), P(None, VOL, SEC), P(None, VOL, SEC), P(), P(), P(SEC, None, VOL)),
        out_specs=(P(None, None, VOL, SEC), P(None, VOL, SEC)),
        check_vma=False,
    )
```

```python
import math

import jax
import jax.numpy as jnp
from jax import lax
from jax.experimental import pallas as pl
from jax.experimental.pallas import tpu as pltpu
from jax.sharding import PartitionSpec as P

SWEEPS = 4
DEEP = SWEEPS - 1

center = 1.0
radius = 0.93

F32 = jnp.float32
BF16 = jnp.bfloat16
SMEM = pl.BlockSpec(memory_space=pltpu.SMEM)
VMEM = pl.BlockSpec(memory_space=pltpu.VMEM)
HBM = pl.BlockSpec(memory_space=pltpu.HBM)

EXC, DEPTH, ROWS, PTS, PARTS = 64, 8, 4, 128, 16
CELLS = DEPTH * ROWS
EDGE = EXC + 16
BULK = DEPTH * DEEP * EXC
SLAB = BULK + 32 + 2 * EDGE
GROUP = 16
WIDE = ROWS + 2 * DEEP
TALL = SWEEPS * ROWS
MINE = EXC // PARTS
PIECE = TALL * (MINE + 1)
RIM = [(d, k) for d in range(SWEEPS - 1, 0, -1) for k in range(d)]

VOL = ("zh", "y", "c")
SEC = ("zl", "x")


def basis_of(perm_ref):
    shape = (PARTS, PARTS)
    own = lax.broadcasted_iota(jnp.int32, shape, 0)
    sector = lax.broadcasted_iota(jnp.int32, shape, 1)
    ids = jnp.zeros(shape, jnp.int32)
    for d in range(PARTS):
        ids = jnp.where(own == d, perm_ref[d], ids)
    half, quarter = PARTS // 2, PARTS // 4
    even = ids <= half
    turn = jnp.where(even, ids, ids - half) * sector
    turn = (turn + jnp.where(even, 0, PARTS - quarter)) & (PARTS - 1)
    value = jnp.zeros(shape, F32)
    for n in range(PARTS):
        value = jnp.where(turn == n, math.cos(2.0 * math.pi * n / PARTS) if n % half != quarter else 0.0, value)
    ends = (ids == 0) | (ids == half)
    return value * jnp.where(ends, math.sqrt(1.0 / PARTS), math.sqrt(2.0 / PARTS))


def lanes_of(shape):
    return lax.broadcasted_iota(jnp.int32, shape, len(shape) - 1)


def source_row(rhs_ref, flux_ref, cell, start, count):
    row = rhs_ref[pl.ds(start * CELLS + cell, count, stride=CELLS), :]
    if cell // ROWS == DEPTH - 1:
        row = row + flux_ref[pl.ds(start * ROWS + cell % ROWS, count, stride=ROWS), :]
    return row


def sigma_of(table_ref, mat):
    sigma = jnp.zeros(mat.shape, F32)
    for m in range(8):
        sigma = jnp.where(mat == float(m), table_ref[m : m + 1, :], sigma)
    return sigma


def by_core(first, second):
    core = lax.axis_index("c")
    pl.when(core == 0)(first)
    pl.when(core == 1)(second)


def share_kernel(rhs_hbm, flux_hbm, mat_hbm, o_ref, rhs_ref, flux_ref, mat_ref, sem):
    copies = [
        pltpu.make_async_copy(rhs_hbm.at[:, pl.ds(CELLS - TALL, TALL), :], rhs_ref, sem.at[0]),
        pltpu.make_async_copy(flux_hbm, flux_ref, sem.at[1]),
        pltpu.make_async_copy(mat_hbm, mat_ref, sem.at[2]),
    ]
    for copy in copies:
        copy.start()
    for copy in copies:
        copy.wait()
    mat = mat_ref[CELLS - TALL : CELLS, :].astype(F32).astype(BF16)
    for e in range(EXC):
        k, own = e // MINE, e % MINE
        f = jnp.concatenate([jnp.zeros((TALL - ROWS, PTS), F32), flux_ref[e * ROWS : (e + 1) * ROWS, :]], 0)
        o_ref[k * PIECE + own * TALL : k * PIECE + (own + 1) * TALL, :] = (rhs_ref[e] + f).astype(BF16)
        if own == 0:
            o_ref[k * PIECE + MINE * TALL : (k + 1) * PIECE, :] = mat


def rim_kernel(x_ref, o_ref, near_ref, far_ref, f_ref):
    f_ref[...] = x_ref[...].astype(F32)
    for r in range(PIECE):
        o_ref[r * PARTS : (r + 1) * PARTS, :] = f_ref[pl.ds(r, PARTS, stride=PIECE), :].astype(BF16)

    def fill(top_ref, bot_ref):
        at = 0
        for d, k in RIM:
            for own in range(MINE + 1):
                top, bot = own * TALL + d * ROWS + k, own * TALL + d * ROWS + ROWS - 1 - k
                top_ref[at : at + PARTS, :] = o_ref[top * PARTS : (top + 1) * PARTS, :]
                bot_ref[at : at + PARTS, :] = o_ref[bot * PARTS : (bot + 1) * PARTS, :]
                at += PARTS

    by_core(lambda: fill(far_ref, near_ref), lambda: fill(near_ref, far_ref))


def take_sides(near_ref, far_ref, next_ref, prev_ref, spans=None):
    def take(a, b):
        for at, count in spans or ((0, next_ref.shape[0]),):
            next_ref[at : at + count, :] = a[at : at + count, :]
            prev_ref[at : at + count, :] = b[at : at + count, :]

    by_core(lambda: take(near_ref, far_ref), lambda: take(far_ref, near_ref))


def trace_kernel(table_ref, x_ref, near_ref, far_ref, o_ref, f_ref, next_ref, prev_ref):
    take_sides(near_ref, far_ref, next_ref, prev_ref)

    def tile(own, d, z):
        if 0 <= z < ROWS:
            ref, at = x_ref, own * TALL + d * ROWS + z
        else:
            ref, k = (prev_ref, -1 - z) if z < 0 else (next_ref, z - ROWS)
            at = RIM.index((d, k)) * (MINE + 1) + own
        return ref[at * PARTS : (at + 1) * PARTS, :].astype(F32)

    top = SWEEPS - 1
    diagonal, inverse = {}, {}
    for d in range(SWEEPS):
        for z in range(-d, ROWS + d):
            diagonal[d, z] = 6.0 + sigma_of(table_ref, tile(MINE, d, z))
            inverse[d, z] = 1.0 / diagonal[d, z]
    lane = lanes_of((PARTS, PTS))

    def sides(v):
        a, b = pltpu.roll(v, 1, 1), pltpu.roll(v, PTS - 1, 1)
        a = jnp.where(lane == 0, pltpu.roll(a, 1, 0), a)
        b = jnp.where(lane == PTS - 1, pltpu.roll(b, PARTS - 1, 0), b)
        return a + b

    sigma_one = center / radius
    traces = []
    for own in range(MINE):
        r = {at: tile(own, *at) for at in diagonal}
        p = {at: r[at] * inverse[at] / center for at in diagonal}
        total = {z: p[top, z] for z in range(ROWS)}
        ratio_now = 1.0 / sigma_one
        for sweep in range(DEEP):
            ratio_next = 1.0 / (2.0 * sigma_one - ratio_now)
            keep, step = ratio_next * ratio_now, 2.0 * ratio_next / radius
            new = {}
            for d in range(sweep + 1, SWEEPS):
                reach = d - sweep - 1
                for z in range(-reach, ROWS + reach):
                    near = p[d - 1, z] + (p[d, z - 1] + p[d, z + 1]) + sides(p[d, z])
                    if d < top:
                        near = near + p[d + 1, z]
                    r[d, z] = r[d, z] - (diagonal[d, z] * p[d, z] - near)
                    new[d, z] = keep * p[d, z] + step * (r[d, z] * inverse[d, z])
            p, ratio_now = new, ratio_next
            total = {z: total[z] + p[top, z] for z in range(ROWS)}
        traces += [total[z].astype(BF16).astype(F32) for z in range(ROWS)]
    y = jnp.dot(table_ref[8:24, :PARTS], jnp.concatenate(traces, 1),
                precision=lax.Precision.HIGHEST, preferred_element_type=F32)
    for k in range(MINE * ROWS):
        f_ref[pl.ds(k, PARTS, stride=MINE * ROWS), :] = y[:, k * PTS : (k + 1) * PTS]
    out = f_ref[...].astype(BF16)
    o_ref[0:256, :] = out
    o_ref[256:512, :] = out


def roll(x, lanes):
    lanes %= PTS
    return pltpu.roll(x, lanes, 1) if lanes else x


def pack_edges(row, cell, low, high):
    lane = lanes_of(row.shape)
    for j in range(DEEP):
        low = jnp.where(lane == 4 * cell + 3 - j, roll(row, 4 * cell + 3 - 2 * j), low)
        high = jnp.where(lane == 4 * cell + j, roll(row, 4 * cell + 2 * j + 1), high)
    return low, high


def edge_kernel(coef_hbm, perm_hbm, rhs_hbm, flux_hbm, mat_hbm, low_ref, high_ref, near_ref, far_ref, table_ref,
                coef_ref, perm_ref, rhs_ref, flux_ref, mat_ref, sem):
    pairs = ((rhs_hbm, rhs_ref), (flux_hbm, flux_ref), (mat_hbm, mat_ref), (coef_hbm, coef_ref), (perm_hbm, perm_ref))
    copies = [pltpu.make_async_copy(*pair, sem.at[k]) for k, pair in enumerate(pairs)]
    for copy in copies:
        copy.start()
    for copy in copies:
        copy.wait()
    by_core(lambda: fill_slabs(rhs_ref, flux_ref, mat_ref, far_ref, near_ref),
            lambda: fill_slabs(rhs_ref, flux_ref, mat_ref, near_ref, far_ref))
    for m in range(8):
        table_ref[m : m + 1, :] = jnp.full((1, PTS), coef_ref[m], F32)
    table_ref[8:24, :PARTS] = basis_of(perm_ref)
    row, col = lax.axis_index("zl"), lax.axis_index("x")
    lane = lanes_of((1, PTS))
    for k in range(4):
        of_owner = table_ref[pl.ds(8 + row * 4 + (col + 4 - k) % 4, 1), :]
        for j in range(4):
            weight = jnp.sum(jnp.where(lane == (row + j) % 4 * 4 + col, of_owner, 0.0), axis=1, keepdims=True)
            table_ref[24 + 4 * k + j : 25 + 4 * k + j, :] = jnp.broadcast_to(weight, (1, PTS))
    sides = (jnp.zeros((EXC, PTS), F32),) * 2
    mats = (jnp.zeros((1, PTS), F32),) * 2
    for cell in range(CELLS):
        sides = pack_edges(source_row(rhs_ref, flux_ref, cell, 0, EXC), cell, *sides)
        mats = pack_edges(mat_ref[cell : cell + 1, :].astype(F32), cell, *mats)
    for ref, side, mat in zip((low_ref, high_ref), sides, mats):
        ref[0:EXC, :] = side.astype(BF16)
        ref[EXC:EDGE, :] = jnp.broadcast_to(mat, (16, PTS)).astype(BF16)


def fill_slabs(rhs_ref, flux_ref, mat_ref, top_ref, bot_ref):
    mtop, mbot = [], []
    for d in range(DEPTH):
        for z in range(ROWS):
            cell = d * ROWS + z
            row = source_row(rhs_ref, flux_ref, cell, 0, EXC).astype(BF16)
            if z < DEEP:
                top_ref[pl.ds((d * DEEP + z) * EXC, EXC), :] = row
            if z >= ROWS - DEEP:
                bot_ref[pl.ds((d * DEEP + z - ROWS + DEEP) * EXC, EXC), :] = row
        mtop.append(mat_ref[d * ROWS : d * ROWS + DEEP, :].astype(F32))
        mbot.append(mat_ref[d * ROWS + ROWS - DEEP : (d + 1) * ROWS, :].astype(F32))
    pad = [jnp.zeros((32 - DEPTH * DEEP, PTS), F32)]
    top_ref[BULK : BULK + 32, :] = jnp.concatenate(mtop + pad, 0).astype(BF16)
    bot_ref[BULK : BULK + 32, :] = jnp.concatenate(mbot + pad, 0).astype(BF16)


def place_edges(halo, right, left, cell, z):
    lane = lanes_of(halo.shape)
    both = jnp.where(lane % 8 < 4, roll(right, 8 * z - 4 * cell), roll(left, 8 * z + 4 - 4 * cell))
    return jnp.where(lane // 8 == z, both, halo)


def sweep_kernel(part, count, table_ref, rhs_hbm, flux_hbm, mat_hbm, right_ref, left_ref, near_ref, far_ref, *refs):
    (out_hbm, dg_ref, iv_ref, r_ref, p0_ref, p1_ref, p2_ref, dgh_ref, ivh_ref, rh_ref, h0_ref, h1_ref, h2_ref,
     next_ref, prev_ref, sol_ref, rhs_ref, flux_ref, mat_ref, sem) = refs[count:]
    rows, at = GROUP * CELLS, part * GROUP
    copies = (pltpu.make_async_copy(mat_hbm, mat_ref, sem.at[0]),
              pltpu.make_async_copy(rhs_hbm.at[pl.ds(part * rows, rows), :], rhs_ref, sem.at[1]),
              pltpu.make_async_copy(flux_hbm.at[pl.ds(at * ROWS, GROUP * ROWS), :], flux_ref, sem.at[2]))
    for copy in copies:
        copy.start()
    spans = [(k * EXC + at, GROUP) for k in range(DEPTH * DEEP)] + [(BULK, SLAB - BULK)]
    take_sides(near_ref, far_ref, next_ref, prev_ref, spans)
    copies[0].wait()

    def where_is(z):
        if z < DEEP:
            return prev_ref, z, z + ROWS - DEEP
        if z >= DEEP + ROWS:
            return next_ref, z - DEEP - ROWS, z - DEEP - ROWS
        return None, None, z - DEEP

    def edges(slab, at, count):
        if slab is None:
            return [ref[pl.ds(at, count), :].astype(F32) for ref in (right_ref, left_ref)]
        return [slab[pl.ds(BULK + 32 + off + at, count), :].astype(F32) for off in (0, EDGE)]

    diagonals, inverses = {}, {}
    for slab in (None, next_ref, prev_ref):
        mat = mat_ref[...] if slab is None else slab[BULK : BULK + 32, :]
        diagonals[id(slab)] = 6.0 + sigma_of(table_ref, mat.astype(F32))
        inverses[id(slab)] = 1.0 / diagonals[id(slab)]
    for d in range(DEPTH):
        halo = jnp.zeros((16, PTS), F32)
        for z in range(WIDE):
            slab, k, own = where_is(z)
            cell = d * ROWS + own
            row = cell if slab is None else d * DEEP + k
            dg_ref[d, z] = jnp.broadcast_to(diagonals[id(slab)][row : row + 1], (8, PTS))
            iv_ref[d, z] = jnp.broadcast_to(inverses[id(slab)][row : row + 1], (8, PTS))
            halo = place_edges(halo, *edges(slab, EXC, 16), cell, z)
        diagonal = 6.0 + sigma_of(table_ref, halo[0:8])
        dgh_ref[d] = diagonal
        ivh_ref[d] = 1.0 / diagonal

    zero = jnp.zeros((GROUP, PTS), F32)
    fields, halos = (p0_ref, p1_ref, p2_ref), (h0_ref, h1_ref, h2_ref)
    for field, halo in zip(fields, halos):
        for d in (0, DEPTH + 1):
            halo[d] = zero
            for z in range(WIDE):
                field[d, z] = zero

    def both(v):
        return jnp.concatenate([v, v], 0)

    lane = lanes_of((GROUP, PTS))
    spot = lane % 8

    def one_group():
        copies[1].wait()
        copies[2].wait()
        packed = {id(slab): edges(slab, at, GROUP) for slab in (None, next_ref, prev_ref)}
        for d in range(DEPTH):
            halo = zero
            for z in range(WIDE):
                slab, k, own = where_is(z)
                cell = d * ROWS + own
                if slab is None:
                    mid = source_row(rhs_ref, flux_ref, cell, 0, GROUP)
                else:
                    mid = slab[pl.ds((d * DEEP + k) * EXC + at, GROUP), :].astype(F32)
                halo = place_edges(halo, *packed[id(slab)], cell, z)
                r_ref[d, z] = mid
                p0_ref[d + 1, z] = mid * both(iv_ref[d, z]) / center
            rh_ref[d] = halo
            h0_ref[d + 1] = halo * both(ivh_ref[d]) / center
        sigma_one = center / radius
        ratio_now = 1.0 / sigma_one
        for sweep in range(DEEP):
            ratio_next = 1.0 / (2.0 * sigma_one - ratio_now)
            keep, step = ratio_next * ratio_now, 2.0 * ratio_next / radius
            last = sweep + 1 == DEEP

            def layer(d, carry, p=fields[sweep], h=halos[sweep], last=last, sweep=sweep, keep=keep, step=step):
                side = h[d + 1]
                ends = zero
                for z in range(1 + sweep, WIDE - 1 - sweep):
                    c = p[d + 1, z]
                    beside = roll(side, -8 * z - 4)
                    total = p[d, z] + p[d + 2, z]
                    total = total + (p[d + 1, z + 1] + p[d + 1, z - 1])
                    total = total + (jnp.where(lane == 0, beside, roll(c, 1)) + jnp.where(lane == PTS - 1, beside, roll(c, -1)))
                    r = r_ref[d, z] - (both(dg_ref[d, z]) * c - total)
                    new = keep * c + step * (r * both(iv_ref[d, z]))
                    if last:
                        out = (p0_ref[d + 1, z] + p1_ref[d + 1, z]) + c + new
                        sol_ref[pl.ds(d * ROWS + z - DEEP, GROUP, stride=CELLS), :] = out
                    else:
                        r_ref[d, z] = r
                        fields[sweep + 1][d + 1, z] = new
                        ends = jnp.where((lane == 8 * z + 3) | (lane == 8 * z + 4), roll(c, 8 * z + 4), ends)
                if not last:
                    total = h[d] + h[d + 2] + (roll(side, 8) + roll(side, -8)) + ends
                    total = total + (jnp.where(spot == 4, 0.0, roll(side, 1)) + jnp.where(spot == 3, 0.0, roll(side, -1)))
                    r = rh_ref[d] - (both(dgh_ref[d]) * side - total)
                    rh_ref[d] = r
                    halos[sweep + 1][d + 1] = keep * side + step * (r * both(ivh_ref[d]))
                return carry

            lax.fori_loop(0, DEPTH, layer, 0, unroll=8)
            ratio_now = ratio_next

    one_group()
    copy = pltpu.make_async_copy(sol_ref, out_hbm.at[pl.ds(part * rows, rows), :], sem.at[3])
    copy.start()
    copy.wait()


def partial_kernel(table_ref, *refs):
    pieces, outs = refs[:4], refs[4:]
    for j in range(4):
        total = jnp.zeros((256, PTS), F32)
        for k in range(4):
            total = total + table_ref[24 + 4 * k + j : 25 + 4 * k + j, :] * pieces[k][...].astype(F32)
        outs[j][...] = total.astype(outs[j].dtype)


def total_kernel(own_ref, *refs):
    total = own_ref[...]
    for ref in refs[:3]:
        total = total + ref[...].astype(F32)
    refs[3][...] = total


def block_kernel(idx_ref, *refs):
    pieces, (w_ref, o_ref, wb_ref, f_ref, sem) = refs[:8], refs[8:]
    deep = ROWS * PTS

    def fetch(k):
        return pltpu.make_async_copy(
            w_ref.at[0, pl.ds(pl.multiple_of(idx_ref[k] * deep, deep), deep), :],
            wb_ref.at[pl.ds(k * deep, deep), :], sem.at[k])

    for k in range(16):
        fetch(k).start()
    for k in range(16):
        f_ref[pl.ds(k * 256, 256), :] = pieces[k // 2][k % 2].astype(F32)
    acc = jnp.zeros((EXC, 512), F32)
    for k in range(16):
        x = jnp.concatenate([f_ref[pl.ds(k * 256 + z, EXC, stride=ROWS), :] for z in range(ROWS)], 1)
        fetch(k).wait()
        acc = acc + jnp.dot(x.astype(BF16), wb_ref[pl.ds(k * deep, deep), :], preferred_element_type=F32)
    for z in range(ROWS):
        f_ref[pl.ds(z, EXC, stride=ROWS), :] = acc[:, z * PTS : (z + 1) * PTS]
    o_ref[...] = f_ref[0:256, :].astype(BF16)


def shape(rows, dtype=BF16, cols=PTS):
    return jax.ShapeDtypeStruct((rows, cols), dtype)


def call(kernel, out, ins, scratch=(), mib=8, **more):
    outs = out if isinstance(out, tuple) else (out,)
    kernel_call = pl.pallas_call(
        kernel, out_shape=outs, in_specs=list(ins), scratch_shapes=list(scratch),
        **({"out_specs": (VMEM,) * len(outs)} | more),
        compiler_params=pltpu.CompilerParams(vmem_limit_bytes=mib << 20))

    def got(*args):
        return kernel_call(*args)

    return got if isinstance(out, tuple) else (lambda *args: got(*args)[0])


def in_hbm(x):
    return pltpu.with_memory_space_constraint(x, pltpu.HBM)


def exchange(x):
    return lax.all_to_all(x.reshape(PARTS, -1, PTS), SEC, 0, 0, tiled=True).reshape(-1, PTS)


def response_of(pair, blocks):
    y, c = lax.axis_index("y"), lax.axis_index("c")

    def rows(k, core):
        return [a * 8 + (y - k) % 4 * 2 + core for a in (0, 1)]

    def swap(v):
        return lax.ppermute(v, "c", [(0, 1), (1, 0)])

    moved = {k: lax.ppermute(pair, "y", [(i, (i + k) % 4) for i in range(4)]) for k in (1, 3, 2)}
    moved[0] = pair
    pieces, index = [], []
    for k in (0, 1, 3, 2):
        pieces += [moved[k], swap(moved[k])]
        index += rows(k, c) + rows(k, 1 - c)
    return call(
        block_kernel, shape(256), [SMEM] + [VMEM] * 8 + [HBM],
        [pltpu.VMEM((8192, 512), BF16), pltpu.VMEM((16 * 256, PTS), F32), pltpu.SemaphoreType.DMA((16,))], mib=16,
    )(jnp.stack(index).astype(jnp.int32), *pieces, in_hbm(blocks))


def per_device(rhs, flux_in, materials, mat_coef, owner_perm, blocks):
    rhs2 = rhs.reshape(EXC * CELLS, PTS)
    flux2 = flux_in.reshape(EXC * ROWS, PTS)
    mat2 = materials.reshape(CELLS, PTS)
    ring = [(i, (i + 1) % 16) for i in range(16)]
    back = [((i + 1) % 16, i) for i in range(16)]
    tie = lax.optimization_barrier

    def near(x):
        return lax.ppermute(x, VOL, [(i, i ^ 1) for i in range(16)])

    def far(x):
        return lax.ppermute(x, VOL, [(i, (i + 1 if i % 2 else i - 1) % 16) for i in range(16)])

    shared = exchange(call(
        share_kernel, shape(PARTS * PIECE), [HBM] * 3,
        [pltpu.VMEM((EXC, TALL, PTS), F32), pltpu.VMEM((EXC * ROWS, PTS), F32), pltpu.VMEM((CELLS, PTS), jnp.int32),
         pltpu.SemaphoreType.DMA((3,))],
    )(*map(in_hbm, (rhs.reshape(EXC, CELLS, PTS), flux2, mat2))))
    low, high, near_slab, far_slab, table = call(
        edge_kernel, (shape(EDGE), shape(EDGE), shape(SLAB), shape(SLAB), shape(40, F32)), [HBM] * 5,
        [pltpu.SMEM((8,), F32), pltpu.SMEM((PARTS,), jnp.int32), pltpu.VMEM((EXC * CELLS, PTS), F32),
         pltpu.VMEM((EXC * ROWS, PTS), F32), pltpu.VMEM((CELLS, PTS), jnp.int32), pltpu.SemaphoreType.DMA((5,))],
    )(*map(in_hbm, (mat_coef, owner_perm, rhs2, flux2, mat2)))
    right = lax.ppermute(low, SEC, back)
    left = lax.ppermute(high, SEC, ring)
    shared, near_slab, far_slab, table = tie((shared, near_slab, far_slab, table))

    rim = shape(len(RIM) * (MINE + 1) * PARTS)
    own, near_rim, far_rim = call(
        rim_kernel, (shape(PARTS * PIECE), rim, rim), [VMEM], [pltpu.VMEM((PARTS * PIECE, PTS), F32)])(shared)
    far_rim, near_rim = far(far_rim), near(near_rim)
    sides = jnp.concatenate([right, left])
    near_slab = lax.dynamic_update_slice(near_slab, sides, (BULK + 32, 0))
    far_slab = lax.dynamic_update_slice(far_slab, sides, (BULK + 32, 0))
    near_slab, far_slab = near(near_slab), far(far_slab)
    harmonics = call(
        trace_kernel, shape(512), [VMEM] * 4, [pltpu.VMEM((256, PTS), F32)] + [pltpu.VMEM(rim.shape, BF16)] * 2,
    )(table, own, near_rim, far_rim)
    pair = lax.all_to_all(harmonics.reshape(32, 16, PTS), ("zh",) + SEC, 0, 0, tiled=True).reshape(2, 256, PTS)
    response = response_of(pair, blocks)

    def turn(x, axis, k):
        return lax.ppermute(x, axis, [(i, (i + k) % 4) for i in range(4)])

    owners = {k: turn(response, "x", k) for k in (1, 3, 2)}
    own_part, *parts = call(
        partial_kernel, (shape(256, F32),) + (shape(256),) * 3, [VMEM] * 5,
    )(table, response, owners[1], owners[2], owners[3])
    parts = [turn(part, "zl", j) for j, part in zip((1, 2, 3), parts)]
    flux = call(total_kernel, shape(256, F32), [VMEM] * 4)(own_part, *parts)

    wide, tall = (DEPTH, WIDE, GROUP, PTS), (DEPTH + 2, WIDE, GROUP, PTS)
    scratch = [(DEPTH, WIDE, 8, PTS)] * 2 + [wide] + [tall] * 3
    scratch += [(DEPTH, 8, PTS)] * 2 + [(DEPTH, GROUP, PTS)] + [(DEPTH + 2, GROUP, PTS)] * 3
    scratch = [pltpu.VMEM(size, F32) for size in scratch] + [pltpu.VMEM((SLAB, PTS), BF16)] * 2
    scratch += [pltpu.VMEM((GROUP * CELLS, PTS), F32)] * 2
    scratch += [pltpu.VMEM((GROUP * ROWS, PTS), F32), pltpu.VMEM((CELLS, PTS), jnp.int32), pltpu.SemaphoreType.DMA((4,))]

    args = (table, *map(in_hbm, (rhs2, flux2, mat2)), right, left, near_slab, far_slab)
    solution = None
    for part in range(EXC // GROUP):
        more = [] if solution is None else [solution]
        specs = [VMEM] + [HBM] * 3 + [VMEM] * 4 + [HBM] * len(more)
        solution = call(
            lambda *refs, part=part, count=len(more): sweep_kernel(part, count, *refs), shape(EXC * CELLS, F32), specs, scratch,
            mib=16, out_specs=(HBM,), input_output_aliases={8: 0} if part else {},
        )(*args, *more)
    return solution.reshape(EXC, DEPTH, ROWS, PTS), flux.reshape(EXC, ROWS, PTS)


def solution(mesh):
    fine = jax.sharding.Mesh(mesh.devices.reshape(2, 4, 2, 4, 4), VOL + SEC)
    return jax.shard_map(
        per_device,
        mesh=fine,
        in_specs=(P(None, None, VOL, SEC), P(None, VOL, SEC), P(None, VOL, SEC), P(), P(), P(SEC, None, VOL)),
        out_specs=(P(None, None, VOL, SEC), P(None, VOL, SEC)),
        check_vma=False,
    )
```
